128 devices in a mesh: row: 4 (over y), col: 8 (over z, core), depth: 4 (over x).
Axes of the slice: x: 4, y: 4, z: 4, core: 2. Of those that a mesh axis runs over, the one named last changes fastest.
Arguments:
- panels: float32 [2, 8192, 512], P(None, ('row', 'depth'), 'col'), may hold values from -6 to 6
- slab: float32 [8192, 4096], P(('row', 'depth'), 'col'), may hold values from -6 to 6
- pivot_one: int32 [512], replicated, may hold values from 512 to 8191, as said below
- pivot_two: int32 [512], replicated, may hold values from 1024 to 8191, as said below
- lower_inv: float32 [2, 512, 512], replicated, may hold values from -1 to 1, as said below
- upper_inv: float32 [2, 512, 512], replicated, may hold values from -1 to 1, as said below
Outputs:
- panels_out: float32 [2, 8192, 512], P(None, ('row', 'depth'), 'col')
- slab_out: float32 [8192, 4096], P(('row', 'depth'), 'col')
The draws below stay inside these ranges and needn't reach their ends.
Inputs may be any that keep to these rules, and one draw needn't show every extreme that they name: `pivot_one`: 512 distinct rows, none among the first 512. `pivot_two`: 512 distinct rows, none among the first 1024. `lower_inv`: each of the two blocks is lower triangular with ones on its diagonal. `upper_inv`: each of the two blocks is upper triangular with a positive diagonal.
All inputs are finite; a program needn't handle non-finite values.
Results may differ from the reference program's by a relative error of at most 0.000075.
Values sent between devices are 32-bit elements; how exact they have to be, the bound alone decides.
No kernel may reach another device: no remote copies, remote signals or barrier semaphores. Data moves between devices by JAX's collectives and lax.ppermute only.
A program may use at most 128 MiB of HBM per device.

```python
import jax
import jax.numpy as jnp
from jax import lax

NB = 512
SLAB = 4096
ROWS = 8192


def draw_pivot_one(key, part):
    shuffled = jax.random.permutation(jax.random.fold_in(key, 11), ROWS - NB)
    return (shuffled[:NB] + NB).astype(jnp.int32)


def draw_pivot_two(key, part):
    shuffled = jax.random.permutation(jax.random.fold_in(key, 12), ROWS - 2 * NB)
    return (shuffled[:NB] + 2 * NB).astype(jnp.int32)


def draw_lower_inv(key, part):
    values = jnp.clip(jax.random.normal(jax.random.fold_in(key, 13), (2, NB, NB), jnp.float32), -1.4, 1.4)
    values = values * (0.7 / NB ** 0.5)
    row_index = jnp.arange(NB, dtype=jnp.int32)[:, None]
    col_index = jnp.arange(NB, dtype=jnp.int32)[None, :]
    strictly_below = (row_index > col_index)[None, :, :]
    on_diagonal = (row_index == col_index)[None, :, :]
    return jnp.where(strictly_below, values, jnp.where(on_diagonal, 1.0, 0.0)).astype(jnp.float32)


def draw_upper_inv(key, part):
    values = jnp.clip(jax.random.normal(jax.random.fold_in(key, 14), (2, NB, NB), jnp.float32), -4.0, 4.0)
    values = values * (0.5 / NB)
    exponent = jax.random.uniform(jax.random.fold_in(key, 15), (2, NB, NB), jnp.float32, jnp.log(0.25), 0.0)
    diagonal = jnp.exp(exponent) / NB ** 0.5
    row_index = jnp.arange(NB, dtype=jnp.int32)[:, None]
    col_index = jnp.arange(NB, dtype=jnp.int32)[None, :]
    strictly_above = (row_index < col_index)[None, :, :]
    on_diagonal = (row_index == col_index)[None, :, :]
    return jnp.where(strictly_above, values, jnp.where(on_diagonal, diagonal, 0.0)).astype(jnp.float32)


def shard_levels(stream_key, dims, cuts, least, largest):
    level = 1.0
    for axis_at, shards_of in cuts:
        draws = jax.random.uniform(jax.random.fold_in(jax.random.fold_in(stream_key, 6), axis_at), (shards_of,), jnp.float32, least / len(cuts), largest / len(cuts))
        level = level * jnp.repeat(jnp.exp(draws), dims[axis_at] // shards_of).reshape((-1,) + (1,) * (len(dims) - 1 - axis_at))
    return level


def scatter_about(own_key, dims, scale, most, pieces=(), kind=jnp.bfloat16):
    factor_of = shard_levels(own_key, dims, pieces, -0.22, 0.18) if pieces else 1.0
    entries = jax.random.normal(own_key, dims, jnp.float32) * scale * factor_of
    return jnp.minimum(jnp.maximum(entries, -most), most).astype(kind)


def setup_inputs(seed: int = 0) -> dict:
    keys = jax.random.split(jax.random.key(seed), 7)
    panels = scatter_about(keys[0], (2, ROWS, NB), 1.0, 6.0, ((1, 16), (2, 8)), jnp.float32)
    slab = scatter_about(keys[1], (ROWS, SLAB), 1.0, 6.0, ((0, 16), (1, 8)), jnp.float32)
    pivot_one = draw_pivot_one(jax.random.fold_in(keys[6], 71), 0)
    pivot_two = draw_pivot_two(jax.random.fold_in(keys[6], 71), 0)
    lower_inv = draw_lower_inv(jax.random.fold_in(keys[6], 71), 0)
    upper_inv = draw_upper_inv(jax.random.fold_in(keys[6], 71), 0)
    return dict(panels=panels, slab=slab, pivot_one=pivot_one, pivot_two=pivot_two, lower_inv=lower_inv, upper_inv=upper_inv)


def fdot(left_side, right_side):
    return jnp.dot(left_side, right_side, preferred_element_type=jnp.float32, precision=lax.Precision.HIGHEST)


def swap_rows(matrix, top_row, pivots):
    height = pivots.shape[0]
    order = jnp.arange(matrix.shape[0], dtype=jnp.int32)
    targets = top_row + jnp.arange(height, dtype=jnp.int32)
    order = order.at[targets].set(pivots.astype(jnp.int32)).at[pivots.astype(jnp.int32)].set(targets)
    return jnp.take(matrix, order, axis=0)


def reference(panels, slab, pivot_one, pivot_two, lower_inv, upper_inv):
    whole = jnp.concatenate([panels[0], panels[1], slab], axis=1)
    first = swap_rows(whole, 0, pivot_one)
    lower_one = fdot(first[NB:, :NB], upper_inv[0])
    upper_one = fdot(lower_inv[0], first[:NB, NB:])
    updated = first[NB:, NB:2 * NB] - fdot(lower_one, upper_one[:, :NB])
    section = jnp.concatenate([lower_one, updated, first[NB:, 2 * NB:]], axis=1)
    second = swap_rows(section, 0, pivot_two - NB)
    lower_two = fdot(second[NB:, NB:2 * NB], upper_inv[1])
    slab_top = second[:NB, 2 * NB:] - fdot(second[:NB, :NB], upper_one[:, NB:])
    upper_two = fdot(lower_inv[1], slab_top)
    left_factor = jnp.concatenate([second[NB:, :NB], lower_two], axis=1)
    right_factor = jnp.concatenate([upper_one[:, NB:], upper_two], axis=0)
    schur = second[NB:, 2 * NB:] - fdot(left_factor, right_factor)
    panel_first = jnp.concatenate([first[:NB, :NB], second[:, :NB]], axis=0)
    panel_second = jnp.concatenate([upper_one[:, :NB], second[:NB, NB:2 * NB], lower_two], axis=0)
    slab_result = jnp.concatenate([upper_one[:, NB:], upper_two, schur], axis=0)
    return jnp.stack([panel_first, panel_second]), slab_result
```

```python
import jax
import jax.numpy as jnp
from jax import lax
from jax.experimental import pallas as pl
from jax.experimental.pallas import tpu as pltpu
from jax.sharding import PartitionSpec as P

NB = 512
CAP = 96
PEERS = 16
SLOTS = PEERS * CAP
RD = ("row", "depth")
F32 = jnp.float32
BF16 = jnp.bfloat16
VMEM = pl.BlockSpec(memory_space=pltpu.VMEM)
SMEM = pl.BlockSpec(memory_space=pltpu.SMEM)


def iota(shape, axis):
    return lax.broadcasted_iota(jnp.int32, shape, axis)


def split2(x):
    high = x.astype(BF16)
    return high, (x - high.astype(F32)).astype(BF16)


def split3(x):
    high = x.astype(BF16)
    rest = x - high.astype(F32)
    middle = rest.astype(BF16)
    return high, middle, (rest - middle.astype(F32)).astype(BF16)


def mm(a, b):
    return jnp.dot(a, b, preferred_element_type=F32)


def dot3(a, b):
    return mm(a[0], b[0]) + (mm(a[0], b[1]) + mm(a[1], b[0]))


def pick(onehot, parts):
    return (mm(onehot, parts[0]) + mm(onehot, parts[1])) + mm(onehot, parts[2])


def column(row):
    return jnp.transpose(jnp.broadcast_to(row, (8, row.shape[1])))[:, :1]


def plan(pivot_one, pivot_two, me):
    j = jnp.arange(NB, dtype=jnp.int32)
    same = pivot_two[:, None] == pivot_one[None, :]
    source_two = jnp.where(
        jnp.any(same, axis=1), jnp.sum(jnp.where(same, j[None, :], 0), axis=1), pivot_two
    )
    again = jnp.any(same, axis=0)
    chain = pivot_one[:, None] == (NB + j)[None, :]
    onward = jnp.sum(jnp.where(chain, pivot_two[None, :], 0), axis=1)
    leaves_one = jnp.where(again, -1, jnp.where(pivot_one < 2 * NB, onward, pivot_one))
    leaves_two = jnp.where(jnp.any(chain, axis=0), -1, pivot_two)
    source = jnp.concatenate([pivot_one, source_two])
    owner = source // NB
    t = jnp.arange(2 * NB, dtype=jnp.int32)
    rank = jnp.sum(((owner[:, None] == owner[None, :]) & (t[None, :] < t[:, None])).astype(jnp.int32), axis=1)
    leaves = jnp.concatenate([leaves_one, leaves_two])
    holder = t // NB
    taker = jnp.where(leaves < 0, -1, leaves // NB)
    key = taker * 2 + holder
    place = jnp.sum(((key[:, None] == key[None, :]) & (t[None, :] < t[:, None])).astype(jnp.int32), axis=1)
    sent = jnp.sum((owner[None, :] == holder[:, None]).astype(jnp.int32), axis=1)
    place = place + sent
    mine = me * NB + j
    hit = source[None, :] == mine[:, None]
    out_rank = jnp.sum(jnp.where(hit, rank[None, :] + 1, 0), axis=1) - 1
    out_taker = jnp.where(me == 0, taker[:NB], jnp.where(me == 1, taker[NB:], -1))
    out_place = jnp.where(me == 0, place[:NB], place[NB:])
    got = leaves[None, :] == mine[:, None]
    in_code = jnp.sum(jnp.where(got, (holder * 4096 + place)[None, :] + 1, 0), axis=1) - 1
    longest = jnp.maximum(jnp.max(rank), jnp.max(jnp.where(leaves < 0, 0, place)))
    return dict(owner=owner, rank=rank, out_rank=out_rank, out_taker=out_taker, out_place=out_place,
                in_code=in_code, rounds=longest // CAP + 1)


def further_rounds(plan_, stacked, lower_inv):
    width = stacked.shape[1]
    k = jnp.arange(CAP, dtype=jnp.int32)
    h = jnp.arange(PEERS, dtype=jnp.int32)

    def turn(state):
        r, top, own = state
        base = r * CAP
        picked = plan_["out_rank"][None, None, :] == (base + k)[None, :, None]
        passed = (plan_["out_taker"][None, None, :] == h[:, None, None]) & (
            plan_["out_place"][None, None, :] == (base + k)[None, :, None]
        )
        which = jnp.sum(jnp.where(picked | passed, jnp.arange(NB, dtype=jnp.int32)[None, None, :], 0), axis=2)
        blocks = jnp.take(stacked, which.reshape(-1), axis=0).reshape(PEERS, CAP, width)
        got = lax.all_to_all(blocks, RD, 0, 0).reshape(SLOTS, width)
        now = (plan_["rank"] // CAP) == r
        at = plan_["owner"] * CAP + plan_["rank"] % CAP
        top = jnp.where(now[:, None], jnp.take(got, at, axis=0), top)
        code = plan_["in_code"]
        place = jnp.maximum(code, 0) % 4096
        at = (jnp.maximum(code, 0) // 4096) * CAP + place % CAP
        now = (code >= 0) & (place // CAP == r)
        own = jnp.where(now[:, None], jnp.take(got, at, axis=0), own)
        return r + 1, top, own

    start = (jnp.int32(1), jnp.zeros((2 * NB, width), F32), jnp.zeros((NB, width), F32))
    _, top, own = lax.while_loop(lambda s: s[0] < plan_["rounds"], turn, start)
    hi = lax.Precision.HIGHEST
    one = jnp.dot(lower_inv[0], top[:NB, 128:], precision=hi, preferred_element_type=F32)
    two = jnp.dot(lower_inv[1], top[NB:, 128:], precision=hi, preferred_element_type=F32)
    panel_extra = jnp.concatenate([top[:, :128], own[:, :128]], axis=0)
    return panel_extra, jnp.stack([one, two, own[:, 128:]])


def pack_kernel(rank_ref, code_ref, rows_ref, out_ref, parts_ref):
    step = pl.program_id(0)

    @pl.when(step == 0)
    def _():
        for n, part in enumerate(split3(rows_ref[...])):
            parts_ref[n] = part

    rank = rank_ref[...]
    code = code_ref[...]
    k = iota((CAP, NB), 0)
    held = k == rank
    blocks = []
    for b in range(4):
        passed = (k + (step * 4 + b) * CAP) == code
        blocks.append(jnp.where(held | passed, 1.0, 0.0).astype(BF16))
    onehot = jnp.concatenate(blocks, axis=0)
    out_ref[...] = pick(onehot, (parts_ref[0], parts_ref[1], parts_ref[2]))


def pack(rank, code, rows):
    width = rows.shape[1]
    return pl.pallas_call(
        pack_kernel,
        grid=(4,),
        in_specs=[
            pl.BlockSpec((1, NB), lambda i: (0, 0)),
            pl.BlockSpec((1, NB), lambda i: (0, 0)),
            pl.BlockSpec((NB, width), lambda i: (0, 0)),
        ],
        out_specs=pl.BlockSpec((4 * CAP, width), lambda i: (i, 0)),
        out_shape=jax.ShapeDtypeStruct((SLOTS, width), F32),
        scratch_shapes=[pltpu.VMEM((3, NB, width), BF16)],
        name="pack_rows",
    )(rank, code, rows)


def slots_of(at_ref, n):
    at = column(at_ref[:, n * NB:(n + 1) * NB])
    return jnp.where(iota((NB, SLOTS), 1) == at, 1.0, 0.0).astype(BF16)


def arrivals(at_ref):
    at = column(at_ref[...])
    onehot = jnp.where(iota((NB, 2 * CAP), 1) == at, 1.0, 0.0).astype(BF16)
    return onehot


def panel_rows_kernel(me_ref, at_ref, in_ref, moved_ref, got_ref, rows_ref, extra_ref, out_ref):
    me = me_ref[0]
    parts = split3(got_ref[...])
    first = pick(slots_of(at_ref, 0), parts) + extra_ref[:NB]
    second = pick(slots_of(at_ref, 1), parts) + extra_ref[NB:2 * NB]
    few = tuple(p[:2 * CAP] for p in parts)
    moved = pick(arrivals(in_ref), few) + extra_ref[2 * NB:]
    own = jnp.where(column(moved_ref[...]) > 0, moved, rows_ref[...])
    own = jnp.where(me == 0, first, jnp.where(me == 1, second, own))
    out_ref[0] = own
    out_ref[1] = jnp.where(iota((NB, 128), 1) < 64, second, first)


def panel_rows(me, at, in_at, moved, got, rows, extra):
    return pl.pallas_call(
        panel_rows_kernel,
        in_specs=[SMEM] + [VMEM] * 6,
        out_specs=VMEM,
        out_shape=jax.ShapeDtypeStruct((2, NB, 128), F32),
        name="panel_rows",
    )(me, at, in_at, moved, got, rows, extra)


def fold_kernel(at_ref, lower_ref, one_ref, two_ref):
    for n, out in enumerate((one_ref, two_ref)):
        onehot = slots_of(at_ref, n)
        high, low = split2(lower_ref[n])
        out[0] = mm(high, onehot).astype(BF16)
        out[1] = mm(low, onehot).astype(BF16)


def fold(at, lower_inv):
    shape = jax.ShapeDtypeStruct((2, NB, SLOTS), BF16)
    return pl.pallas_call(
        fold_kernel, in_specs=[VMEM] * 2, out_specs=[VMEM] * 2, out_shape=[shape, shape], name="fold_slots"
    )(at, lower_inv)


def panel_math_kernel(me_ref, own0, own1, own2, own3, oth0, oth1, oth2, oth3, lower_ref, upper_ref,
                      left_ref, pout_ref, gath, src):
    me, core, z = me_ref[0], me_ref[1], me_ref[2]
    for s, (a, b) in enumerate(((own0, oth0), (own1, oth1), (own2, oth2), (own3, oth3))):
        zz = lax.rem(z + 4 - s, 4)
        gath[core, zz] = a[...]
        gath[1 - core, zz] = b[...]
    left_half = iota((NB, 128), 1) < 64

    def panel(kind, half):
        blocks = []
        for zz in range(4):
            a, b = gath[kind, zz, 0], gath[kind, zz, 1]
            if half == 0:
                blocks.append(jnp.where(left_half, a, pltpu.roll(b, 64, 1)))
            else:
                blocks.append(jnp.where(left_half, pltpu.roll(a, 64, 1), b))
        return jnp.concatenate(blocks, axis=1)

    own_one, own_two = panel(0, 0), panel(0, 1)
    top_two_one, top_one_two = panel(1, 0), panel(1, 1)
    upper_one_inv = split2(upper_ref[0])
    lower_kept = dot3(split2(own_one), upper_one_inv)
    lower_top = dot3(split2(top_two_one), upper_one_inv)
    upper_panel = dot3(split2(lower_ref[0]), split2(top_one_two))
    kept_parts = split2(lower_kept)
    updated = own_two - dot3(kept_parts, split2(upper_panel))
    lower_two = dot3(split2(updated), split2(upper_ref[1]))
    left_ref[0], left_ref[1] = kept_parts
    left_ref[2], left_ref[3] = split2(lower_two)
    left_ref[4], left_ref[5] = split2(dot3(split2(lower_ref[1]), split2(lower_top)))
    src[0] = jnp.where(me == 0, own_one, lower_kept)
    src[1] = jnp.where(me == 0, upper_panel, jnp.where(me == 1, updated, lower_two))
    at = pl.multiple_of(z * 128, 128)
    one = src[0, :, pl.ds(at, 128)]
    two = src[1, :, pl.ds(at, 128)]
    pout_ref[...] = jnp.where(
        core == 0,
        jnp.where(left_half, one, pltpu.roll(two, 64, 1)),
        jnp.where(left_half, pltpu.roll(one, 64, 1), two),
    )


def panel_math(where, own, other, lower_inv, upper_inv):
    return pl.pallas_call(
        panel_math_kernel,
        in_specs=[SMEM] + [VMEM] * 10,
        out_specs=[VMEM] * 2,
        out_shape=[jax.ShapeDtypeStruct((6, NB, NB), BF16), jax.ShapeDtypeStruct((NB, 128), F32)],
        scratch_shapes=[pltpu.VMEM((2, 4, 2, NB, 128), F32), pltpu.VMEM((2, NB, NB), F32)],
        name="panel_math",
    )(where, *own, *other, lower_inv, upper_inv)


def slab_kernel(me_ref, in_ref, moved_ref, got_ref, rows_ref, extra_ref, one_ref, two_ref, left_ref, out_ref):
    me = me_ref[0]
    got = split2(got_ref[...])
    upper_one = dot3((one_ref[0], one_ref[1]), got) + extra_ref[0]
    one = split2(upper_one)
    upper_two = (dot3((two_ref[0], two_ref[1]), got) - dot3((left_ref[4], left_ref[5]), one)) + extra_ref[1]

    @pl.when(me == 0)
    def _():
        out_ref[...] = upper_one

    @pl.when(me == 1)
    def _():
        out_ref[...] = upper_two

    @pl.when(me > 1)
    def _():
        few = split3(got_ref[:2 * CAP])
        moved = pick(arrivals(in_ref), few) + extra_ref[2]
        own = jnp.where(column(moved_ref[...]) > 0, moved, rows_ref[...])
        two = split2(upper_two)
        out_ref[...] = own - dot3((left_ref[0], left_ref[1]), one) - dot3((left_ref[2], left_ref[3]), two)


def slab_math(where, in_at, moved, got, rows, extra, one, two, left):
    wide = 256
    whole = lambda *shape: pl.BlockSpec(shape, lambda i: (0,) * len(shape))
    return pl.pallas_call(
        slab_kernel,
        grid=(NB // wide,),
        in_specs=[
            SMEM,
            whole(1, NB),
            whole(1, NB),
            pl.BlockSpec((SLOTS, wide), lambda i: (0, i)),
            pl.BlockSpec((NB, wide), lambda i: (0, i)),
            pl.BlockSpec((3, NB, wide), lambda i: (0, 0, i)),
            whole(2, NB, SLOTS),
            whole(2, NB, SLOTS),
            whole(6, NB, NB),
        ],
        out_specs=pl.BlockSpec((NB, wide), lambda i: (0, i)),
        out_shape=jax.ShapeDtypeStruct((NB, NB), F32),
        name="slab_math",
    )(where, in_at, moved, got, rows, extra, one, two, left)


def exchange(blocks):
    width = blocks.shape[1]
    return lax.all_to_all(blocks.reshape(PEERS, CAP, width), RD, 0, 0).reshape(SLOTS, width)


def partner(x):
    return lax.ppermute(x, "col", [(c, c ^ 1) for c in range(8)])


def shift(x, by):
    return lax.ppermute(x, "col", [(c, (c // 2 + by) % 4 * 2 + c % 2) for c in range(8)])


def local(panels, slab, pivot_one, pivot_two, lower_inv, upper_inv):
    me = lax.axis_index(RD)
    col = lax.axis_index("col")
    core, z = col % 2, col // 2
    where = jnp.stack([me, core, z, z]).astype(jnp.int32)
    steps = plan(pivot_one, pivot_two, me)
    row = lambda v: v.astype(jnp.int32).reshape(1, -1)
    fits = steps["rank"] < CAP
    at = row(jnp.where(fits, steps["owner"] * CAP + steps["rank"], -1))
    out_code = row(
        jnp.where(
            (steps["out_taker"] >= 0) & (steps["out_place"] < CAP),
            steps["out_taker"] * CAP + steps["out_place"],
            -1,
        )
    )
    out_rank = row(steps["out_rank"])
    code = steps["in_code"]
    moved = row(code >= 0)
    place = code % 4096
    in_at = row(jnp.where((code >= 0) & (place < CAP), (code // 4096) * CAP + place, -1))

    panel = jnp.concatenate([panels[0], panels[1]], axis=1)
    extra_panel, extra_slab = lax.cond(
        steps["rounds"] > 1,
        lambda: further_rounds(steps, jnp.concatenate([panel, slab], axis=1), lower_inv),
        lambda: (jnp.zeros((3 * NB, 128), F32), jnp.zeros((3, NB, NB), F32)),
    )
    got_panel = exchange(pack(out_rank, out_code, panel))
    got_slab = exchange(pack(out_rank, out_code, slab))
    both = panel_rows(where, at, in_at, moved, got_panel, panel, extra_panel)
    theirs = partner(jnp.where(core == 0, both[1], both[0]))
    mine = jnp.where(core == 0, both[0], both[1])
    pair = jnp.stack([jnp.where(core == 0, mine, theirs), jnp.where(core == 0, theirs, mine)])
    own = [pair] + [shift(pair, by) for by in (1, 2, 3)]
    other = [partner(x) for x in own]
    one, two = fold(at, lower_inv)
    left, panel_out = panel_math(where, own, other, lower_inv, upper_inv)
    slab_out = slab_math(where, in_at, moved, got_slab, slab, extra_slab, one, two, left)
    return jnp.stack([panel_out[:, :64], panel_out[:, 64:]]), slab_out


def solution(mesh):
    placed = (P(None, RD, "col"), P(RD, "col"), P(), P(), P(), P())
    return jax.shard_map(
        local,
        mesh=mesh,
        in_specs=placed,
        out_specs=(P(None, RD, "col"), P(RD, "col")),
        check_vma=False,
    )
```

```python
import jax
import jax.numpy as jnp
from jax import lax
from jax.experimental import pallas as pl
from jax.experimental.pallas import tpu as pltpu
from jax.sharding import PartitionSpec as P


NB = 512
CAP = 96
PEERS = 16
SLOTS = PEERS * CAP
HALF = (NB + 2 * CAP) // 2
RD = ("row", "depth")
F32 = jnp.float32
BF16 = jnp.bfloat16
VMEM = pl.BlockSpec(memory_space=pltpu.VMEM)
ANY = pl.BlockSpec(memory_space=pl.ANY)
SMEM = pl.BlockSpec(memory_space=pltpu.SMEM)


def iota(shape, axis):
    return lax.broadcasted_iota(jnp.int32, shape, axis)


def split2(x):
    high = x.astype(BF16)
    return high, (x - high.astype(F32)).astype(BF16)


def split3(x):
    high = x.astype(BF16)
    rest = x - high.astype(F32)
    middle = rest.astype(BF16)
    return high, middle, (rest - middle.astype(F32)).astype(BF16)


def mm(a, b):
    return jnp.dot(a, b, preferred_element_type=F32)


def dot3(a, b):
    return mm(a[0], b[0]) + (mm(a[0], b[1]) + mm(a[1], b[0]))


def pick(onehot, parts):
    return (mm(onehot, parts[0]) + mm(onehot, parts[1])) + mm(onehot, parts[2])


def pick_t(onehot, parts):
    dots = [lax.dot_general(onehot, p, (((1,), (1,)), ((), ())), preferred_element_type=F32) for p in parts]
    return (dots[0] + dots[1]) + dots[2]


def column(row):
    return jnp.transpose(jnp.broadcast_to(row, (8, row.shape[1])))[:, :1]


def running(x):
    lane = iota(x.shape, 1)
    by = 1
    while by < x.shape[1]:
        x = x + jnp.where(lane >= by, pltpu.roll(x, by, 1), 0.0)
        by *= 2
    return x


def down(mask, value):
    return jnp.sum(jnp.where(mask, value, 0.0), axis=0, keepdims=True)


def blocks_onehot(rank, code, first, count):
    k = iota((CAP, NB), 0)
    held = k == rank
    blocks = [
        jnp.where(held | ((k + (first + b) * CAP) == code), 1.0, 0.0).astype(BF16) for b in range(count)
    ]
    return jnp.concatenate(blocks, axis=0)


def plan_kernel(where_ref, one_ref, two_ref, panel_ref, at_ref, codes_ref, every_ref, most_ref, out_ref):
    me = where_ref[0]
    one, two = one_ref[...].astype(F32), two_ref[...].astype(F32)
    one_c, two_c = column(one), column(two)
    lane = iota((1, NB), 1).astype(F32)
    sub = iota((NB, 1), 0).astype(F32)
    hit = down(one_c == two, sub + 1.0)
    source = jnp.concatenate([one, jnp.where(hit > 0, hit - 1.0, two)], axis=1)
    again = down(two_c == one, 1.0) > 0
    taken = down(one_c == lane + NB, 1.0) > 0
    onward = down(sub + NB == one, two_c)
    leaves = (
        jnp.where(again, -1.0, jnp.where(one < 2 * NB, onward, one)),
        jnp.where(taken, -1.0, two),
    )
    owner = source.astype(jnp.int32) >> 9
    owners = jnp.where(iota((PEERS, 2 * NB), 0) == owner, 1.0, 0.0)
    count = running(owners)
    rank = jnp.sum(owners * count, axis=0, keepdims=True) - 1.0
    takers = [v.astype(jnp.int32) >> 9 for v in leaves]
    taker_rows = jnp.concatenate([jnp.where(iota((PEERS, NB), 0) == t, 1.0, 0.0) for t in takers], axis=0)
    taker_count = taker_rows * running(taker_rows)
    most = jnp.max(rank)
    out_codes, in_codes, out_every, in_every = [], [], [], []
    for q in range(2):
        sent = count[q:q + 1, 2 * NB - 1:]
        place = jnp.sum(taker_count[q * PEERS:(q + 1) * PEERS], axis=0, keepdims=True) - 1.0 + sent
        place = place.astype(jnp.int32)
        most = jnp.maximum(most, jnp.max(jnp.where(takers[q] < 0, 0, place).astype(F32)))
        fits = place < CAP
        out_codes.append(jnp.where((takers[q] >= 0) & fits, takers[q] * CAP + place, -1))
        in_codes.append(jnp.where(fits, place + (q * CAP + 2), 1).astype(F32))
        out_every.append(jnp.where(takers[q] >= 0, takers[q] * 4096 + place, -1))
        in_every.append((place + (q * 4096 + 1)).astype(F32))
    most_ref[0] = most.astype(jnp.int32)
    mine = lane + (me * NB).astype(F32)
    out_rank = (down(column(source) == mine, column(rank) + 1.0) - 1.0).astype(jnp.int32)
    out_code = jnp.where(me == 0, out_codes[0], jnp.where(me == 1, out_codes[1], -1))
    code = jnp.where(me == 0, out_every[0], jnp.where(me == 1, out_every[1], -1))
    hit = column(jnp.concatenate(leaves, axis=1)) == mine
    in_code = down(hit, column(jnp.concatenate(in_codes, axis=1)))
    rank = rank.astype(jnp.int32)
    at_ref[...] = jnp.where(rank < CAP, owner * CAP + rank, -1)
    codes_ref[0:1] = out_rank
    codes_ref[1:2] = out_code
    codes_ref[2:3] = in_code.astype(jnp.int32) - 2
    codes_ref[3:4] = code
    codes_ref[4:5] = code
    codes_ref[5:8] = jnp.zeros((3, NB), jnp.int32)
    every_ref[:, :2 * NB] = owner * 4096 + rank
    every_ref[:, 2 * NB:] = down(hit, column(jnp.concatenate(in_every, axis=1))).astype(jnp.int32) - 1
    parts = split3(panel_ref[...])
    for c in range(4):
        onehot = blocks_onehot(out_rank, out_code, 4 * c, 4)
        out_ref[4 * c * CAP:4 * (c + 1) * CAP] = pick_t(onehot, parts)


def make_plan(where, pivot_one, pivot_two, panel_t):
    return pl.pallas_call(
        plan_kernel,
        in_specs=[SMEM] + [VMEM] * 3,
        out_specs=[VMEM, VMEM, VMEM, SMEM, VMEM],
        out_shape=[
            jax.ShapeDtypeStruct((1, 2 * NB), jnp.int32),
            jax.ShapeDtypeStruct((8, NB), jnp.int32),
            jax.ShapeDtypeStruct((1, 3 * NB), jnp.int32),
            jax.ShapeDtypeStruct((1,), jnp.int32),
            jax.ShapeDtypeStruct((SLOTS, 128), F32),
        ],
        name="make_plan",
    )(where, pivot_one.reshape(1, NB), pivot_two.reshape(1, NB), panel_t)


def pack_kernel(codes_ref, rows_ref, out_ref, parts_ref):
    step = pl.program_id(0)

    @pl.when(step == 0)
    def _():
        for n, part in enumerate(split3(rows_ref[...])):
            parts_ref[n] = part

    onehot = blocks_onehot(codes_ref[0:1], codes_ref[1:2], step * 4, 4)
    out_ref[...] = pick(onehot, (parts_ref[0], parts_ref[1], parts_ref[2]))


def pack(codes, rows):
    width = rows.shape[1]
    return pl.pallas_call(
        pack_kernel,
        grid=(4,),
        in_specs=[pl.BlockSpec((8, NB), lambda i: (0, 0)), pl.BlockSpec((NB, width), lambda i: (0, 0))],
        out_specs=pl.BlockSpec((4 * CAP, width), lambda i: (i, 0)),
        out_shape=jax.ShapeDtypeStruct((SLOTS, width), F32),
        scratch_shapes=[pltpu.VMEM((3, NB, width), BF16)],
        name="pack_rows",
    )(codes, rows)


def slots_of(at_ref, n):
    at = column(at_ref[:, n * NB:(n + 1) * NB])
    return jnp.where(iota((NB, SLOTS), 1) == at, 1.0, 0.0).astype(BF16)


def arrivals(codes_ref):
    code = column(codes_ref[2:3])
    return jnp.where(iota((NB, 2 * CAP), 1) == code, 1.0, 0.0).astype(BF16), code > -2


def late(flag_ref, extra_ref, buffer, sem):
    @pl.when(flag_ref[0] < CAP)
    def _():
        buffer[...] = jnp.zeros_like(buffer)

    @pl.when(flag_ref[0] >= CAP)
    def _():
        copy = pltpu.make_async_copy(extra_ref, buffer, sem)
        copy.start()
        copy.wait()

    return buffer


def panel_rows_kernel(where_ref, flag_ref, at_ref, got_ref, extra_ref, keep_ref, send_ref, tops_ref, more, sem):
    core = where_ref[1]
    more = late(flag_ref, extra_ref.at[:2 * NB, :128], more, sem)
    parts = split3(got_ref[...])
    first = pick(slots_of(at_ref, 0), parts) + more[:NB]
    second = pick(slots_of(at_ref, 1), parts) + more[NB:]
    left = iota((NB, 128), 1) < 64
    tops_ref[...] = jnp.where(left, first, second)
    swapped = jnp.where(left, second, first)
    upper = swapped[:HALF]
    lower = jnp.concatenate([swapped[HALF:], got_ref[:2 * CAP]], axis=0)
    keep_ref[...] = jnp.where(core == 0, upper, lower)
    send_ref[...] = jnp.where(core == 0, lower, upper)


def panel_rows(where, flag, at, got, extra):
    half = jax.ShapeDtypeStruct((HALF, 128), F32)
    return pl.pallas_call(
        panel_rows_kernel,
        in_specs=[SMEM] * 2 + [VMEM] * 2 + [ANY],
        out_specs=[VMEM] * 3,
        out_shape=[half, half, jax.ShapeDtypeStruct((NB, 128), F32)],
        scratch_shapes=[pltpu.VMEM((2 * NB, 128), F32), pltpu.SemaphoreType.DMA],
        name="panel_rows",
    )(where, flag, at, got, extra)


def fold_kernel(at_ref, lower_ref, one_ref, two_ref):
    for n, out in enumerate((one_ref, two_ref)):
        onehot = slots_of(at_ref, n)
        high, low = split2(lower_ref[n])
        out[0] = mm(high, onehot).astype(BF16)
        out[1] = mm(low, onehot).astype(BF16)


def fold(at, lower_inv):
    shape = jax.ShapeDtypeStruct((2, NB, SLOTS), BF16)
    return pl.pallas_call(
        fold_kernel, in_specs=[VMEM] * 2, out_specs=[VMEM] * 2, out_shape=[shape, shape], name="fold_slots"
    )(at, lower_inv)


def own_panels_kernel(where_ref, *refs):
    pieces, out_ref, gath = refs[:8], refs[8], refs[9]
    col = where_ref[3]
    for m in range(8):
        gath[lax.bitwise_xor(col, m)] = pieces[m][...]
    for n in range(2):
        whole = jnp.concatenate([gath[c, 64 * n:64 * (n + 1)] for c in range(8)], axis=0)
        out_ref[n] = jnp.transpose(whole)


def own_panels(where, pieces):
    return pl.pallas_call(
        own_panels_kernel,
        in_specs=[SMEM] + [VMEM] * 8,
        out_specs=VMEM,
        out_shape=jax.ShapeDtypeStruct((2, NB, NB), F32),
        scratch_shapes=[pltpu.VMEM((8, 128, NB), F32)],
        name="own_panels",
    )(where, *pieces)


def panel_math_kernel(where_ref, flag_ref, codes_ref, tops_ref, whole_ref, extra_ref, k0, k1, k2, k3, p0, p1, p2, p3,
                      lower_ref, upper_ref, left_ref, pout_ref, gath, src, more, sem):
    me, core, z = where_ref[0], where_ref[1], where_ref[2]
    for s, (a, b) in enumerate(((k0, p0), (k1, p1), (k2, p2), (k3, p3))):
        zz = lax.rem(z + 4 - s, 4)
        gath[core, zz] = a[...]
        gath[1 - core, zz] = b[...]
    more = late(flag_ref, extra_ref, more, sem)
    left = iota((2 * HALF, 128), 1) < 64
    ones, twos = [], []
    for zz in range(4):
        a = jnp.concatenate([gath[0, zz, :HALF], gath[1, zz, HALF:]], axis=0)
        b = jnp.concatenate([gath[0, zz, HALF:], gath[1, zz, :HALF]], axis=0)
        ones.append(jnp.where(left, a, pltpu.roll(b, 64, 1)))
        twos.append(jnp.where(left, pltpu.roll(a, 64, 1), b))
    in_one, in_two = jnp.concatenate(ones, axis=1), jnp.concatenate(twos, axis=1)
    onehot, moved = arrivals(codes_ref)
    top_two_one, top_one_two = in_one[:NB], in_two[:NB]
    own_one = jnp.where(moved, pick(onehot, split3(in_one[NB:])) + more[0], whole_ref[0])
    own_two = jnp.where(moved, pick(onehot, split3(in_two[NB:])) + more[1], whole_ref[1])
    own_one = jnp.where(me == 1, top_two_one, own_one)
    own_two = jnp.where(me == 1, 0.0, own_two)
    upper_one_inv = split2(upper_ref[0])
    lower_kept = dot3(split2(own_one), upper_one_inv)
    lower_top = dot3(split2(top_two_one), upper_one_inv)
    upper_panel = dot3(split2(lower_ref[0]), split2(top_one_two))
    kept_parts = split2(lower_kept)
    updated = own_two - dot3(kept_parts, split2(upper_panel))
    lower_two = dot3(split2(updated), split2(upper_ref[1]))
    left_ref[0], left_ref[1] = kept_parts
    left_ref[2], left_ref[3] = split2(lower_two)
    left_ref[4], left_ref[5] = split2(dot3(split2(lower_ref[1]), split2(lower_top)))
    src[0] = lower_kept
    src[1] = jnp.where(me == 0, upper_panel, jnp.where(me == 1, updated, lower_two))
    at = pl.multiple_of(z * 128, 128)
    one = src[0, :, pl.ds(at, 128)]
    two = src[1, :, pl.ds(at, 128)]
    left = iota((NB, 128), 1) < 64
    mine = jnp.where(
        core == 0,
        jnp.where(left, one, pltpu.roll(two, 64, 1)),
        jnp.where(left, pltpu.roll(one, 64, 1), two),
    )
    tops = tops_ref[...]
    mine = jnp.where(left & (me == 0), tops, mine)
    mine = jnp.where(jnp.logical_not(left) & (me == 1), tops + mine, mine)
    pout_ref[...] = jnp.transpose(mine)


def panel_math(where, flag, codes, tops, whole, extra, kept, other, lower_inv, upper_inv):
    return pl.pallas_call(
        panel_math_kernel,
        in_specs=[SMEM] * 2 + [VMEM] * 3 + [ANY] + [VMEM] * 10,
        out_specs=[VMEM] * 2,
        out_shape=[jax.ShapeDtypeStruct((6, NB, NB), BF16), jax.ShapeDtypeStruct((128, NB), F32)],
        scratch_shapes=[
            pltpu.VMEM((2, 4, 2 * HALF, 128), F32),
            pltpu.VMEM((2, NB, NB), F32),
            pltpu.VMEM((2, NB, NB), F32),
            pltpu.SemaphoreType.DMA,
        ],
        name="panel_math",
    )(where, flag, codes, tops, whole, extra, *kept, *other, lower_inv, upper_inv)


WIDE = 256


def slab_kernel(where_ref, flag_ref, codes_ref, got_ref, rows_ref, extra_ref, one_ref, two_ref, left_ref, out_ref,
                more, sem):
    me = where_ref[0]
    at = pl.multiple_of(pl.program_id(0) * WIDE, WIDE)
    more = late(flag_ref, extra_ref.at[:, pl.ds(at, WIDE)], more, sem)
    got = split2(got_ref[...])
    upper_one = dot3((one_ref[0], one_ref[1]), got) + more[:NB]
    one = split2(upper_one)
    upper_two = (dot3((two_ref[0], two_ref[1]), got) - dot3((left_ref[4], left_ref[5]), one)) + more[NB:2 * NB]

    @pl.when(me == 0)
    def _():
        out_ref[...] = upper_one

    @pl.when(me == 1)
    def _():
        out_ref[...] = upper_two

    @pl.when(me > 1)
    def _():
        onehot, moved = arrivals(codes_ref)
        own = jnp.where(moved, pick(onehot, split3(got_ref[:2 * CAP])) + more[2 * NB:], rows_ref[...])
        two = split2(upper_two)
        out_ref[...] = own - dot3((left_ref[0], left_ref[1]), one) - dot3((left_ref[2], left_ref[3]), two)


def slab_math(where, flag, codes, got, rows, extra, one, two, left):
    whole = lambda *shape: pl.BlockSpec(shape, lambda i: (0,) * len(shape))
    return pl.pallas_call(
        slab_kernel,
        grid=(NB // WIDE,),
        in_specs=[
            SMEM,
            SMEM,
            whole(8, NB),
            pl.BlockSpec((SLOTS, WIDE), lambda i: (0, i)),
            pl.BlockSpec((NB, WIDE), lambda i: (0, i)),
            ANY,
            whole(2, NB, SLOTS),
            whole(2, NB, SLOTS),
            whole(6, NB, NB),
        ],
        out_specs=pl.BlockSpec((NB, WIDE), lambda i: (0, i)),
        out_shape=jax.ShapeDtypeStruct((NB, NB), F32),
        scratch_shapes=[pltpu.VMEM((3 * NB, WIDE), F32), pltpu.SemaphoreType.DMA],
        name="slab_math",
    )(where, flag, codes, got, rows, extra, one, two, left)


def mark_kernel(in_ref, out_ref):
    out_ref[0] = in_ref[0]


def mark(x):
    return pl.pallas_call(
        mark_kernel, in_specs=[SMEM], out_specs=SMEM, out_shape=jax.ShapeDtypeStruct((1,), jnp.int32), name="mark"
    )(x)


def exchange(blocks):
    width = blocks.shape[1]
    return lax.all_to_all(blocks.reshape(PEERS, CAP, width), RD, 0, 0).reshape(SLOTS, width)


def unused_kernel(*refs):
    pass


def unwritten(*shapes):
    return pl.pallas_call(
        unused_kernel,
        out_specs=[ANY] * len(shapes),
        out_shape=[jax.ShapeDtypeStruct(shape, F32) for shape in shapes],
        name="unwritten",
    )()


def late_pack_kernel(base_ref, codes_ref, panel_ref, rows_ref, out_ref):
    k = iota((CAP, NB), 0) + base_ref[0]
    picked = (k == codes_ref[0:1]) | ((k + pl.program_id(0) * 4096) == codes_ref[4:5])
    onehot = jnp.where(picked, 1.0, 0.0).astype(BF16)
    out_ref[:, :128] = pick_t(onehot, split3(panel_ref[...]))
    out_ref[:, 128:] = pick(onehot, split3(rows_ref[...]))


def late_pack(base, codes, panel_t, slab):
    whole = lambda *shape: pl.BlockSpec(shape, lambda i: (0,) * len(shape))
    return pl.pallas_call(
        late_pack_kernel,
        grid=(PEERS,),
        in_specs=[SMEM, whole(8, NB), whole(128, NB), whole(NB, NB)],
        out_specs=pl.BlockSpec((CAP, 128 + NB), lambda i: (i, 0)),
        out_shape=jax.ShapeDtypeStruct((SLOTS, 128 + NB), F32),
        name="late_pack",
    )(base, codes, panel_t, slab)


def late_place_kernel(base_ref, every_ref, got_ref, old_ref, out_ref):
    code = column(every_ref[...])
    place = (code & 4095) - base_ref[0]
    now = (code >= 0) & (place >= 0) & (place < CAP)
    at = jnp.where(now, (code >> 12) * CAP + place, -1)
    onehot = jnp.where(iota((128, SLOTS), 1) == at, 1.0, 0.0).astype(BF16)
    old = jnp.where(base_ref[0] == CAP, 0.0, old_ref[...])
    out_ref[...] = jnp.where(now, pick(onehot, split3(got_ref[...])), old)


def late_place(base, every, got, old):
    block = pl.BlockSpec((128, 128 + NB), lambda i: (i, 0))
    return pl.pallas_call(
        late_place_kernel,
        grid=(12,),
        in_specs=[
            SMEM,
            pl.BlockSpec((1, 128), lambda i: (0, i)),
            pl.BlockSpec((SLOTS, 128 + NB), lambda i: (0, 0)),
            block,
        ],
        out_specs=block,
        out_shape=jax.ShapeDtypeStruct((3 * NB, 128 + NB), F32),
        name="late_place",
    )(base, every, got, old)


def late_product_kernel(lower_ref, rows_ref, out_ref):
    n = pl.program_id(0)

    @pl.when(n < 8)
    def _():
        out_ref[...] = dot3(split2(lower_ref[0]), split2(rows_ref[:, 128:]))

    @pl.when(n >= 8)
    def _():
        at = pl.multiple_of(lax.rem(n, 4) * 128, 128)
        out_ref[...] = rows_ref[pl.ds(at, 128), 128:]


def late_product(lower_inv, rows):
    return pl.pallas_call(
        late_product_kernel,
        grid=(12,),
        in_specs=[
            pl.BlockSpec((1, 128, NB), lambda i: (lax.min(i // 4, 1), i % 4, 0)),
            pl.BlockSpec((NB, 128 + NB), lambda i: (i // 4, 0)),
        ],
        out_specs=pl.BlockSpec((128, NB), lambda i: (i, 0)),
        out_shape=jax.ShapeDtypeStruct((3 * NB, NB), F32),
        name="late_product",
    )(lower_inv, rows)


def late_panel_kernel(in_ref, out_ref):
    left = iota((NB, 128), 1) < 64
    a, b = in_ref[0], in_ref[1]
    out_ref[0] = jnp.where(left, a, pltpu.roll(b, 64, 1))
    out_ref[1] = jnp.where(left, pltpu.roll(a, 64, 1), b)


def late_panel(pieces):
    return pl.pallas_call(
        late_panel_kernel,
        grid=(4,),
        in_specs=[pl.BlockSpec((2, NB, 128), lambda i: (i, 0, 0))],
        out_specs=pl.BlockSpec((2, NB, 128), lambda i: (0, 0, i)),
        out_shape=jax.ShapeDtypeStruct((2, NB, NB), F32),
        name="late_panel",
    )(pieces)


def late_exchange(blocks, me):
    ring = [(i, (i + 1) % PEERS) for i in range(PEERS)]

    def turn(t, state):
        held, got = state
        mine = lax.dynamic_slice_in_dim(held, me * CAP, CAP, 0)
        got = lax.dynamic_update_slice_in_dim(got, mine, (me - t) % PEERS * CAP, 0)
        return lax.ppermute(held, RD, ring), got

    return lax.fori_loop(0, PEERS, turn, (blocks, jnp.zeros(blocks.shape, F32)))[1]


def late_gather(rows, col):
    ring = [(i, (i + 1) % 8) for i in range(8)]

    def turn(t, state):
        held, got = state
        got = lax.dynamic_update_slice_in_dim(got, held[None], (col - t) % 8, 0)
        return lax.ppermute(held, "col", ring), got

    return lax.fori_loop(0, 8, turn, (rows, jnp.zeros((8, *rows.shape), F32)))[1]


def further_rounds(most, codes, every, panel_t, slab, lower_inv, me, col):
    def turn(state):
        r, rows = state[:2]
        base = (r * CAP).reshape(1)
        got = late_exchange(late_pack(base, codes, panel_t, slab), me)
        rows = late_place(base, every, got, rows)
        wide = late_panel(late_gather(rows[2 * NB:, :128], col))
        return r + 1, rows, wide, late_product(lower_inv, rows)

    start = (jnp.int32(1), *unwritten((3 * NB, 128 + NB), (2, NB, NB), (3 * NB, NB)))
    return lax.while_loop(lambda s: s[0] * CAP <= most, turn, start)[1:]


def partner(x, by=1):
    return lax.ppermute(x, "col", [(c, c ^ by) for c in range(8)])


def shift(x, by):
    return lax.ppermute(x, "col", [(c, (c // 2 + by) % 4 * 2 + c % 2) for c in range(8)])


def body(panels, slab, pivot_one, pivot_two, lower_inv, upper_inv):
    me = lax.axis_index(RD)
    col = lax.axis_index("col")
    where = jnp.stack([me, col % 2, col // 2, col]).astype(jnp.int32)
    panel_t = jnp.swapaxes(panels, 1, 2).reshape(128, NB)
    at, codes, every, most, blocks = make_plan(where, pivot_one, pivot_two, panel_t)
    got_panel = exchange(blocks)
    pieces = [panel_t] + [partner(panel_t, by) for by in range(1, 8)]
    whole = own_panels(where, pieces)
    blocks = pack(codes, slab)
    most = mark(most)
    late_rows, late_own, late_slab = further_rounds(most[0], codes, every, panel_t, slab, lower_inv, me, col)
    got_slab = exchange(blocks)
    keep, send, tops = panel_rows(where, most, at, got_panel, late_rows)
    pair = jnp.concatenate([keep, partner(send)], axis=0)
    shifted = [shift(pair, by) for by in (1, 2, 3)]
    one, two = fold(at, lower_inv)
    shifted, one, two = lax.optimization_barrier((shifted, one, two))
    kept = [pair] + shifted
    other = [partner(x) for x in kept]
    left, panel_out = panel_math(where, most, codes, tops, whole, late_own, kept, other, lower_inv, upper_inv)
    slab_out = slab_math(where, most, codes, got_slab, slab, late_slab, one, two, left)
    return jnp.swapaxes(panel_out.reshape(2, 64, NB), 1, 2), slab_out


def solution(mesh):
    placed = (P(None, RD, "col"), P(RD, "col"), P(), P(), P(), P())
    return jax.shard_map(
        body,
        mesh=mesh,
        in_specs=placed,
        out_specs=(P(None, RD, "col"), P(RD, "col")),
        check_vma=False,
    )
```

```python
import jax
import jax.numpy as jnp
from jax import lax
from jax.experimental import pallas as pl
from jax.experimental.pallas import tpu as pltpu
from jax.sharding import PartitionSpec as P


NB = 512
CAP = 96
PEERS = 16
SLOTS = PEERS * CAP
HALF = (NB + 2 * CAP) // 2
RD = ("row", "depth")
F32 = jnp.float32
BF16 = jnp.bfloat16
VMEM = pl.BlockSpec(memory_space=pltpu.VMEM)
ANY = pl.BlockSpec(memory_space=pl.ANY)
SMEM = pl.BlockSpec(memory_space=pltpu.SMEM)


def iota(shape, axis):
    return lax.broadcasted_iota(jnp.int32, shape, axis)


def split2(x):
    high = x.astype(BF16)
    return high, (x - high.astype(F32)).astype(BF16)


def mm(a, b):
    return jnp.dot(a, b, preferred_element_type=F32)


def dot3(a, b):
    both = jnp.concatenate([a[0], a[1]], axis=1)
    return mm(both, jnp.concatenate([b[0], b[0]], axis=0)) + mm(a[0], b[1])


def cut(parts, rows, cols):
    return tuple(p[rows, cols] for p in parts)


FIRST, LAST, ALL = slice(0, NB // 2), slice(NB // 2, NB), slice(None)


def dot3_upper(a, b):
    left = dot3(cut(a, ALL, FIRST), cut(b, FIRST, FIRST))
    return jnp.concatenate([left, dot3(a, cut(b, ALL, LAST))], axis=1)


def dot3_lower(a, b):
    top = dot3(cut(a, FIRST, FIRST), cut(b, FIRST, ALL))
    return jnp.concatenate([top, dot3(cut(a, LAST, ALL), b)], axis=0)


def pick(onehot, parts):
    width = parts[0].shape[1]
    if width > 128:
        return mm(onehot, parts[0]) + mm(onehot, parts[1])
    both = mm(onehot, jnp.concatenate(parts, axis=1))
    return both[:, :width] + both[:, width:]


def pick_t(onehot, parts):
    both = jnp.concatenate(parts, axis=0)
    both = lax.dot_general(onehot, both, (((1,), (1,)), ((), ())), preferred_element_type=F32)
    return both[:, :128] + both[:, 128:]


def in_first(code):
    return jnp.where((code & 4095) < CAP, (code >> 12) * CAP + (code & 4095), -1)


def column(row):
    return jnp.transpose(jnp.broadcast_to(row, (8, row.shape[1])))[:, :1]


def running(x):
    lane = iota(x.shape, 1)
    by = 1
    while by < x.shape[1]:
        x = x + jnp.where(lane >= by, pltpu.roll(x, by, 1), 0.0)
        by *= 2
    return x


def down(mask, value):
    return jnp.sum(jnp.where(mask, value, 0.0), axis=0, keepdims=True)


def blocks_onehot(rank, code, first, count):
    k = iota((CAP, NB), 0)
    held = k == rank
    code = in_first(code)
    blocks = [
        jnp.where(held | ((k + (first + b) * CAP) == code), 1.0, 0.0).astype(BF16) for b in range(count)
    ]
    return jnp.concatenate(blocks, axis=0)


def plan_kernel(where_ref, one_ref, two_ref, panel_ref, codes_ref, every_ref, most_ref, out_ref):
    me = where_ref[0]
    one, two = one_ref[...].astype(F32), two_ref[...].astype(F32)
    one_c, two_c = column(one), column(two)
    lane = iota((1, NB), 1).astype(F32)
    sub = iota((NB, 1), 0).astype(F32)
    hit = down(one_c == two, sub + 1.0)
    source = jnp.concatenate([one, jnp.where(hit > 0, hit - 1.0, two)], axis=1)
    again = down(two_c == one, 1.0) > 0
    taken = down(one_c == lane + NB, 1.0) > 0
    onward = down(sub + NB == one, two_c)
    leaves = (
        jnp.where(again, -1.0, jnp.where(one < 2 * NB, onward, one)),
        jnp.where(taken, -1.0, two),
    )
    owner = source.astype(jnp.int32) >> 9
    owners = jnp.where(iota((PEERS, 2 * NB), 0) == owner, 1.0, 0.0)
    count = running(owners)
    rank = jnp.sum(owners * count, axis=0, keepdims=True) - 1.0
    takers = [v.astype(jnp.int32) >> 9 for v in leaves]
    taker_rows = jnp.concatenate([jnp.where(iota((PEERS, NB), 0) == t, 1.0, 0.0) for t in takers], axis=0)
    taker_count = taker_rows * running(taker_rows)
    most = jnp.max(rank)
    out_codes, in_codes = [], []
    for q in range(2):
        sent = count[q:q + 1, 2 * NB - 1:]
        place = jnp.sum(taker_count[q * PEERS:(q + 1) * PEERS], axis=0, keepdims=True) - 1.0 + sent
        place = place.astype(jnp.int32)
        most = jnp.maximum(most, jnp.max(jnp.where(takers[q] < 0, 0, place).astype(F32)))
        out_codes.append(jnp.where(takers[q] >= 0, takers[q] * 4096 + place, -1))
        in_codes.append((place + (q * 4096 + 1)).astype(F32))
    most_ref[0] = most.astype(jnp.int32)
    mine = lane + (me * NB).astype(F32)
    out_rank = (down(column(source) == mine, column(rank) + 1.0) - 1.0).astype(jnp.int32)
    out_code = jnp.where(me == 0, out_codes[0], jnp.where(me == 1, out_codes[1], -1))
    hit = column(jnp.concatenate(leaves, axis=1)) == mine
    in_code = down(hit, column(jnp.concatenate(in_codes, axis=1))).astype(jnp.int32) - 1
    codes_ref[0:1] = out_rank
    codes_ref[1:2] = out_code
    codes_ref[2:8] = jnp.zeros((6, NB), jnp.int32)
    every_ref[:, :2 * NB] = owner * 4096 + rank.astype(jnp.int32)
    every_ref[:, 2 * NB:] = in_code
    parts = split2(panel_ref[...])
    for c in range(4):
        onehot = blocks_onehot(out_rank, out_code, 4 * c, 4)
        out_ref[4 * c * CAP:4 * (c + 1) * CAP] = pick_t(onehot, parts)


def make_plan(where, pivot_one, pivot_two, panel_t):
    return pl.pallas_call(
        plan_kernel,
        in_specs=[SMEM] + [VMEM] * 3,
        out_specs=[VMEM, VMEM, SMEM, VMEM],
        out_shape=[
            jax.ShapeDtypeStruct((8, NB), jnp.int32),
            jax.ShapeDtypeStruct((1, 3 * NB), jnp.int32),
            jax.ShapeDtypeStruct((1,), jnp.int32),
            jax.ShapeDtypeStruct((SLOTS, 128), F32),
        ],
        name="make_plan",
    )(where, pivot_one.reshape(1, NB), pivot_two.reshape(1, NB), panel_t)


def pack_kernel(codes_ref, rows_ref, out_ref, parts_ref):
    step = pl.program_id(0)

    @pl.when(step == 0)
    def _():
        for n, part in enumerate(split2(rows_ref[...])):
            parts_ref[n] = part

    onehot = blocks_onehot(codes_ref[0:1], codes_ref[1:2], step * 4, 4)
    out_ref[...] = pick(onehot, (parts_ref[0], parts_ref[1], parts_ref[2]))


def pack(codes, rows):
    width = rows.shape[1]
    return pl.pallas_call(
        pack_kernel,
        grid=(4,),
        in_specs=[pl.BlockSpec((8, NB), lambda i: (0, 0)), pl.BlockSpec((NB, width), lambda i: (0, 0))],
        out_specs=pl.BlockSpec((4 * CAP, width), lambda i: (i, 0)),
        out_shape=jax.ShapeDtypeStruct((SLOTS, width), F32),
        scratch_shapes=[pltpu.VMEM((3, NB, width), BF16)],
        name="pack_rows",
    )(codes, rows)


def slots_of(at_ref, n):
    at = column(in_first(at_ref[:, n * NB:(n + 1) * NB]))
    return jnp.where(iota((NB, SLOTS), 1) == at, 1.0, 0.0).astype(BF16)


def arrivals(at_ref):
    code = at_ref[:, 2 * NB:]
    at = column(in_first(code))
    return jnp.where(iota((NB, 2 * CAP), 1) == at, 1.0, 0.0).astype(BF16), column(code) >= 0


def late(flag_ref, extra_ref, buffer, sem):
    @pl.when(flag_ref[0] < CAP)
    def _():
        buffer[...] = jnp.zeros_like(buffer)

    @pl.when(flag_ref[0] >= CAP)
    def _():
        copy = pltpu.make_async_copy(extra_ref, buffer, sem)
        copy.start()
        copy.wait()

    return buffer


def panel_rows_kernel(where_ref, flag_ref, at_ref, got_ref, extra_ref, keep_ref, send_ref, tops_ref, more, sem):
    core = where_ref[1]
    more = late(flag_ref, extra_ref.at[:2 * NB, :128], more, sem)
    parts = split2(got_ref[...])
    first = pick(slots_of(at_ref, 0), parts) + more[:NB]
    second = pick(slots_of(at_ref, 1), parts) + more[NB:]
    left = iota((NB, 128), 1) < 64
    tops_ref[...] = jnp.where(left, first, second)
    swapped = jnp.where(left, second, first)
    upper = swapped[:HALF]
    lower = jnp.concatenate([swapped[HALF:], got_ref[:2 * CAP]], axis=0)
    keep_ref[...] = jnp.where(core == 0, upper, lower)
    send_ref[...] = jnp.where(core == 0, lower, upper)


def panel_rows(where, flag, at, got, extra):
    half = jax.ShapeDtypeStruct((HALF, 128), F32)
    return pl.pallas_call(
        panel_rows_kernel,
        in_specs=[SMEM] * 2 + [VMEM] * 2 + [ANY],
        out_specs=[VMEM] * 3,
        out_shape=[half, half, jax.ShapeDtypeStruct((NB, 128), F32)],
        scratch_shapes=[pltpu.VMEM((2 * NB, 128), F32), pltpu.SemaphoreType.DMA],
        name="panel_rows",
    )(where, flag, at, got, extra)


def fold_kernel(at_ref, lower_ref, one_ref, two_ref):
    for n, out in enumerate((one_ref, two_ref)):
        onehot = slots_of(at_ref, n)
        high, low = split2(lower_ref[n])
        out[0] = mm(high, onehot).astype(BF16)
        out[1] = mm(low, onehot).astype(BF16)


def fold(at, lower_inv):
    shape = jax.ShapeDtypeStruct((2, NB, SLOTS), BF16)
    return pl.pallas_call(
        fold_kernel, in_specs=[VMEM] * 2, out_specs=[VMEM] * 2, out_shape=[shape, shape], name="fold_slots"
    )(at, lower_inv)


def own_panels_kernel(where_ref, p0, p1, p2, p3, out_ref, gath):
    core, z = where_ref[1], where_ref[2]
    for s, piece in enumerate((p0, p1, p2, p3)):
        zz = lax.rem(z + 4 - s, 4)
        gath[zz, core] = piece[:128]
        gath[zz, 1 - core] = piece[128:]
    for n in range(2):
        half = [gath[c // 2, c % 2, 64 * n:64 * (n + 1)] for c in range(8)]
        out_ref[n] = jnp.transpose(jnp.concatenate(half, axis=0))


def own_panels(where, pieces):
    return pl.pallas_call(
        own_panels_kernel,
        in_specs=[SMEM] + [VMEM] * 4,
        out_specs=VMEM,
        out_shape=jax.ShapeDtypeStruct((2, NB, NB), F32),
        scratch_shapes=[pltpu.VMEM((4, 2, 128, NB), F32)],
        name="own_panels",
    )(where, *pieces)


def panel_math_kernel(where_ref, flag_ref, at_ref, tops_ref, whole_ref, extra_ref, k0, k1, k2, k3, p0, p1, p2, p3,
                      lower_ref, upper_ref, left_ref, pout_ref, gath, src, more, sem):
    me, core, z = where_ref[0], where_ref[1], where_ref[2]
    for s, (a, b) in enumerate(((k0, p0), (k1, p1), (k2, p2), (k3, p3))):
        zz = lax.rem(z + 4 - s, 4)
        gath[core, zz] = a[...]
        gath[1 - core, zz] = b[...]
    more = late(flag_ref, extra_ref, more, sem)
    left = iota((2 * HALF, 128), 1) < 64
    ones, twos = [], []
    for zz in range(4):
        a = jnp.concatenate([gath[0, zz, :HALF], gath[1, zz, HALF:]], axis=0)
        b = jnp.concatenate([gath[0, zz, HALF:], gath[1, zz, :HALF]], axis=0)
        ones.append(jnp.where(left, a, pltpu.roll(b, 64, 1)))
        twos.append(jnp.where(left, pltpu.roll(a, 64, 1), b))
    in_one, in_two = jnp.concatenate(ones, axis=1), jnp.concatenate(twos, axis=1)
    onehot, moved = arrivals(at_ref)
    top_two_one, top_one_two = in_one[:NB], in_two[:NB]
    own_one = jnp.where(moved, pick(onehot, split2(in_one[NB:])) + more[0], whole_ref[0])
    own_two = jnp.where(moved, pick(onehot, split2(in_two[NB:])) + more[1], whole_ref[1])
    own_one = jnp.where(me == 1, top_two_one, own_one)
    own_two = jnp.where(me == 1, 0.0, own_two)
    upper_one_inv = split2(upper_ref[0])
    lower_kept = dot3_upper(split2(own_one), upper_one_inv)
    lower_top = dot3_upper(split2(top_two_one), upper_one_inv)
    upper_panel = dot3_lower(split2(lower_ref[0]), split2(top_one_two))
    kept_parts = split2(lower_kept)
    updated = own_two - dot3(kept_parts, split2(upper_panel))
    lower_two = dot3_upper(split2(updated), split2(upper_ref[1]))
    left_ref[0], left_ref[1] = kept_parts
    left_ref[2], left_ref[3] = split2(lower_two)
    left_ref[4], left_ref[5] = split2(dot3_lower(split2(lower_ref[1]), split2(lower_top)))
    src[0] = lower_kept
    src[1] = jnp.where(me == 0, upper_panel, jnp.where(me == 1, updated, lower_two))
    at = pl.multiple_of(z * 128, 128)
    one = src[0, :, pl.ds(at, 128)]
    two = src[1, :, pl.ds(at, 128)]
    left = iota((NB, 128), 1) < 64
    mine = jnp.where(
        core == 0,
        jnp.where(left, one, pltpu.roll(two, 64, 1)),
        jnp.where(left, pltpu.roll(one, 64, 1), two),
    )
    tops = tops_ref[...]
    mine = jnp.where(left & (me == 0), tops, mine)
    mine = jnp.where(jnp.logical_not(left) & (me == 1), tops + mine, mine)
    pout_ref[...] = jnp.transpose(mine)


def panel_math(where, flag, at, tops, whole, extra, kept, other, lower_inv, upper_inv):
    return pl.pallas_call(
        panel_math_kernel,
        in_specs=[SMEM] * 2 + [VMEM] * 3 + [ANY] + [VMEM] * 10,
        out_specs=[VMEM] * 2,
        out_shape=[jax.ShapeDtypeStruct((6, NB, NB), BF16), jax.ShapeDtypeStruct((128, NB), F32)],
        scratch_shapes=[
            pltpu.VMEM((2, 4, 2 * HALF, 128), F32),
            pltpu.VMEM((2, NB, NB), F32),
            pltpu.VMEM((2, NB, NB), F32),
            pltpu.SemaphoreType.DMA,
        ],
        name="panel_math",
    )(where, flag, at, tops, whole, extra, *kept, *other, lower_inv, upper_inv)


WIDE = 256


def slab_kernel(where_ref, flag_ref, at_ref, got_ref, rows_ref, extra_ref, one_ref, two_ref, left_ref, out_ref,
                more, sem):
    me = where_ref[0]
    at = pl.multiple_of(pl.program_id(0) * WIDE, WIDE)
    more = late(flag_ref, extra_ref.at[:, pl.ds(at, WIDE)], more, sem)
    got = split2(got_ref[...])
    upper_one = dot3((one_ref[0], one_ref[1]), got) + more[:NB]
    one = split2(upper_one)
    upper_two = (dot3((two_ref[0], two_ref[1]), got) - dot3((left_ref[4], left_ref[5]), one)) + more[NB:2 * NB]

    @pl.when(me == 0)
    def _():
        out_ref[...] = upper_one

    @pl.when(me == 1)
    def _():
        out_ref[...] = upper_two

    @pl.when(me > 1)
    def _():
        onehot, moved = arrivals(at_ref)
        own = jnp.where(moved, pick(onehot, split2(got_ref[:2 * CAP])) + more[2 * NB:], rows_ref[...])
        two = split2(upper_two)
        out_ref[...] = own - dot3((left_ref[0], left_ref[1]), one) - dot3((left_ref[2], left_ref[3]), two)


def slab_math(where, flag, at, got, rows, extra, one, two, left):
    whole = lambda *shape: pl.BlockSpec(shape, lambda i: (0,) * len(shape))
    return pl.pallas_call(
        slab_kernel,
        grid=(NB // WIDE,),
        in_specs=[
            SMEM,
            SMEM,
            whole(1, 3 * NB),
            pl.BlockSpec((SLOTS, WIDE), lambda i: (0, i)),
            pl.BlockSpec((NB, WIDE), lambda i: (0, i)),
            ANY,
            whole(2, NB, SLOTS),
            whole(2, NB, SLOTS),
            whole(6, NB, NB),
        ],
        out_specs=pl.BlockSpec((NB, WIDE), lambda i: (0, i)),
        out_shape=jax.ShapeDtypeStruct((NB, NB), F32),
        scratch_shapes=[pltpu.VMEM((3 * NB, WIDE), F32), pltpu.SemaphoreType.DMA],
        name="slab_math",
    )(where, flag, at, got, rows, extra, one, two, left)


def mark_kernel(in_ref, out_ref):
    out_ref[0] = in_ref[0]


def mark(x):
    return pl.pallas_call(
        mark_kernel, in_specs=[SMEM], out_specs=SMEM, out_shape=jax.ShapeDtypeStruct((1,), jnp.int32), name="mark"
    )(x)


def exchange(blocks):
    width = blocks.shape[1]
    return lax.all_to_all(blocks.reshape(PEERS, CAP, width), RD, 0, 0).reshape(SLOTS, width)


def unused_kernel(*refs):
    pass


def unwritten(*shapes):
    return pl.pallas_call(
        unused_kernel,
        out_specs=[ANY] * len(shapes),
        out_shape=[jax.ShapeDtypeStruct(shape, F32) for shape in shapes],
        name="unwritten",
    )()


def late_pack_kernel(base_ref, codes_ref, panel_ref, rows_ref, out_ref):
    k = iota((CAP, NB), 0) + base_ref[0]
    picked = (k == codes_ref[0:1]) | ((k + pl.program_id(0) * 4096) == codes_ref[1:2])
    onehot = jnp.where(picked, 1.0, 0.0).astype(BF16)
    out_ref[:, :128] = pick_t(onehot, split2(panel_ref[...]))
    out_ref[:, 128:] = pick(onehot, split2(rows_ref[...]))


def late_pack(base, codes, panel_t, slab):
    whole = lambda *shape: pl.BlockSpec(shape, lambda i: (0,) * len(shape))
    return pl.pallas_call(
        late_pack_kernel,
        grid=(PEERS,),
        in_specs=[SMEM, whole(8, NB), whole(128, NB), whole(NB, NB)],
        out_specs=pl.BlockSpec((CAP, 128 + NB), lambda i: (i, 0)),
        out_shape=jax.ShapeDtypeStruct((SLOTS, 128 + NB), F32),
        name="late_pack",
    )(base, codes, panel_t, slab)


def late_place_kernel(base_ref, every_ref, got_ref, old_ref, out_ref):
    code = column(every_ref[...])
    place = (code & 4095) - base_ref[0]
    now = (code >= 0) & (place >= 0) & (place < CAP)
    at = jnp.where(now, (code >> 12) * CAP + place, -1)
    onehot = jnp.where(iota((128, SLOTS), 1) == at, 1.0, 0.0).astype(BF16)
    old = jnp.where(base_ref[0] == CAP, 0.0, old_ref[...])
    out_ref[...] = jnp.where(now, pick(onehot, split2(got_ref[...])), old)


def late_place(base, every, got, old):
    block = pl.BlockSpec((128, 128 + NB), lambda i: (i, 0))
    return pl.pallas_call(
        late_place_kernel,
        grid=(12,),
        in_specs=[
            SMEM,
            pl.BlockSpec((1, 128), lambda i: (0, i)),
            pl.BlockSpec((SLOTS, 128 + NB), lambda i: (0, 0)),
            block,
        ],
        out_specs=block,
        out_shape=jax.ShapeDtypeStruct((3 * NB, 128 + NB), F32),
        name="late_place",
    )(base, every, got, old)


def late_product_kernel(lower_ref, rows_ref, out_ref):
    n = pl.program_id(0)

    @pl.when(n < 8)
    def _():
        out_ref[...] = dot3(split2(lower_ref[0]), split2(rows_ref[:, 128:]))

    @pl.when(n >= 8)
    def _():
        at = pl.multiple_of(lax.rem(n, 4) * 128, 128)
        out_ref[...] = rows_ref[pl.ds(at, 128), 128:]


def late_product(lower_inv, rows):
    return pl.pallas_call(
        late_product_kernel,
        grid=(12,),
        in_specs=[
            pl.BlockSpec((1, 128, NB), lambda i: (lax.min(i // 4, 1), i % 4, 0)),
            pl.BlockSpec((NB, 128 + NB), lambda i: (i // 4, 0)),
        ],
        out_specs=pl.BlockSpec((128, NB), lambda i: (i, 0)),
        out_shape=jax.ShapeDtypeStruct((3 * NB, NB), F32),
        name="late_product",
    )(lower_inv, rows)


def late_panel_kernel(in_ref, out_ref):
    left = iota((NB, 128), 1) < 64
    a, b = in_ref[0], in_ref[1]
    out_ref[0] = jnp.where(left, a, pltpu.roll(b, 64, 1))
    out_ref[1] = jnp.where(left, pltpu.roll(a, 64, 1), b)


def late_panel(pieces):
    return pl.pallas_call(
        late_panel_kernel,
        grid=(4,),
        in_specs=[pl.BlockSpec((2, NB, 128), lambda i: (i, 0, 0))],
        out_specs=pl.BlockSpec((2, NB, 128), lambda i: (0, 0, i)),
        out_shape=jax.ShapeDtypeStruct((2, NB, NB), F32),
        name="late_panel",
    )(pieces)


def late_exchange(blocks, me):
    ring = [(i, (i + 1) % PEERS) for i in range(PEERS)]

    def turn(t, state):
        held, got = state
        mine = lax.dynamic_slice_in_dim(held, me * CAP, CAP, 0)
        got = lax.dynamic_update_slice_in_dim(got, mine, (me - t) % PEERS * CAP, 0)
        return lax.ppermute(held, RD, ring), got

    return lax.fori_loop(0, PEERS, turn, (blocks, jnp.zeros(blocks.shape, F32)))[1]


def late_gather(rows, col):
    ring = [(i, (i + 1) % 8) for i in range(8)]

    def turn(t, state):
        held, got = state
        got = lax.dynamic_update_slice_in_dim(got, held[None], (col - t) % 8, 0)
        return lax.ppermute(held, "col", ring), got

    return lax.fori_loop(0, 8, turn, (rows, jnp.zeros((8, *rows.shape), F32)))[1]


def further_rounds(most, codes, every, panel_t, slab, lower_inv, me, col):
    def turn(state):
        r, rows = state[:2]
        base = (r * CAP).reshape(1)
        got = late_exchange(late_pack(base, codes, panel_t, slab), me)
        rows = late_place(base, every, got, rows)
        wide = late_panel(late_gather(rows[2 * NB:, :128], col))
        return r + 1, rows, wide, late_product(lower_inv, rows)

    start = (jnp.int32(1), *unwritten((3 * NB, 128 + NB), (2, NB, NB), (3 * NB, NB)))
    return lax.while_loop(lambda s: s[0] * CAP <= most, turn, start)[1:]


def partner(x):
    return lax.ppermute(x, "col", [(c, c ^ 1) for c in range(8)])


def shift(x, by):
    return lax.ppermute(x, "col", [(c, (c // 2 + by) % 4 * 2 + c % 2) for c in range(8)])


def body(panels, slab, pivot_one, pivot_two, lower_inv, upper_inv):
    me = lax.axis_index(RD)
    col = lax.axis_index("col")
    where = jnp.stack([me, col % 2, col // 2, col]).astype(jnp.int32)
    panel_t = jnp.swapaxes(panels, 1, 2).reshape(128, NB)
    panel_pair = jnp.concatenate([panel_t, partner(panel_t)], axis=0)
    codes, every, most, blocks = make_plan(where, pivot_one, pivot_two, panel_t)
    got_panel = exchange(blocks)
    pieces = [panel_pair] + [shift(panel_pair, by) for by in (1, 2, 3)]
    whole = own_panels(where, pieces)
    blocks = pack(codes, slab)
    most = mark(most)
    late_rows, late_own, late_slab = further_rounds(most[0], codes, every, panel_t, slab, lower_inv, me, col)
    got_slab = exchange(blocks)
    keep, send, tops = panel_rows(where, most, every, got_panel, late_rows)
    pair = jnp.concatenate([keep, partner(send)], axis=0)
    shifted = [shift(pair, by) for by in (1, 2, 3)]
    one, two = fold(every, lower_inv)
    shifted, one, two = lax.optimization_barrier((shifted, one, two))
    kept = [pair] + shifted
    other = [partner(x) for x in kept]
    left, panel_out = panel_math(where, most, every, tops, whole, late_own, kept, other, lower_inv, upper_inv)
    slab_out = slab_math(where, most, every, got_slab, slab, late_slab, one, two, left)
    return jnp.swapaxes(panel_out.reshape(2, 64, NB), 1, 2), slab_out


def solution(mesh):
    placed = (P(None, RD, "col"), P(RD, "col"), P(), P(), P(), P())
    return jax.shard_map(
        body,
        mesh=mesh,
        in_specs=placed,
        out_specs=(P(None, RD, "col"), P(RD, "col")),
        check_vma=False,
    )
```

```python
import jax
import jax.numpy as jnp
from jax import lax
from jax.experimental import pallas as pl
from jax.experimental.pallas import tpu as pltpu
from jax.sharding import PartitionSpec as P


NB = 512
CAP = 96
PEERS = 16
SLOTS = PEERS * CAP
SOME = 64
FEW = PEERS * SOME
HALF = (NB + 2 * CAP) // 2
RD = ("row", "depth")
F32 = jnp.float32
BF16 = jnp.bfloat16
VMEM = pl.BlockSpec(memory_space=pltpu.VMEM)
ANY = pl.BlockSpec(memory_space=pl.ANY)
SMEM = pl.BlockSpec(memory_space=pltpu.SMEM)


def iota(shape, axis):
    return lax.broadcasted_iota(jnp.int32, shape, axis)


def split2(x):
    high = x.astype(BF16)
    return high, (x - high.astype(F32)).astype(BF16)


def mm(a, b):
    return jnp.dot(a, b, preferred_element_type=F32)


def dot3(a, b):
    both = jnp.concatenate([a[0], a[1]], axis=1)
    return mm(both, jnp.concatenate([b[0], b[0]], axis=0)) + mm(a[0], b[1])


def cut(parts, rows, cols):
    return tuple(p[rows, cols] for p in parts)


FIRST, LAST, ALL = slice(0, NB // 2), slice(NB // 2, NB), slice(None)


def dot3_upper(a, b):
    left = dot3(cut(a, ALL, FIRST), cut(b, FIRST, FIRST))
    return jnp.concatenate([left, dot3(a, cut(b, ALL, LAST))], axis=1)


def dot3_lower(a, b):
    top = dot3(cut(a, FIRST, FIRST), cut(b, FIRST, ALL))
    return jnp.concatenate([top, dot3(cut(a, LAST, ALL), b)], axis=0)


def pick(onehot, parts):
    width = parts[0].shape[1]
    if width > 128:
        return mm(onehot, parts[0]) + mm(onehot, parts[1])
    both = mm(onehot, jnp.concatenate(parts, axis=1))
    return both[:, :width] + both[:, width:]


def pick_t(onehot, parts):
    both = jnp.concatenate(parts, axis=0)
    both = lax.dot_general(onehot, both, (((1,), (1,)), ((), ())), preferred_element_type=F32)
    return both[:, :128] + both[:, 128:]


def in_first(code):
    return jnp.where((code & 4095) < CAP, (code >> 12) * CAP + (code & 4095), -1)


def column(row):
    return jnp.transpose(jnp.broadcast_to(row, (8, row.shape[1])))[:, :1]


def running(x):
    n = x.shape[1]
    upto = jnp.where(iota((n, n), 0) <= iota((n, n), 1), 1.0, 0.0).astype(BF16)
    return mm(x.astype(BF16), upto)


def down(mask, value):
    return jnp.sum(jnp.where(mask, value, 0.0), axis=0, keepdims=True)


def blocks_onehot(rank, code, first, count):
    k = iota((CAP, NB), 0)
    held = k == rank
    code = in_first(code)
    blocks = [
        jnp.where(held | ((k + (first + b) * CAP) == code), 1.0, 0.0).astype(BF16) for b in range(count)
    ]
    return jnp.concatenate(blocks, axis=0)


def plan_kernel(where_ref, one_ref, two_ref, panel_ref, codes_ref, every_ref, most_ref, out_ref):
    me = where_ref[0]
    one, two = one_ref[...].astype(F32), two_ref[...].astype(F32)
    one_c, two_c = column(one), column(two)
    lane = iota((1, NB), 1).astype(F32)
    sub = iota((NB, 1), 0).astype(F32)
    hit = down(one_c == two, sub + 1.0)
    source = jnp.concatenate([one, jnp.where(hit > 0, hit - 1.0, two)], axis=1)
    again = down(two_c == one, 1.0) > 0
    taken = down(one_c == lane + NB, 1.0) > 0
    onward = down(sub + NB == one, two_c)
    leaves = (
        jnp.where(again, -1.0, jnp.where(one < 2 * NB, onward, one)),
        jnp.where(taken, -1.0, two),
    )
    owner = source.astype(jnp.int32) >> 9
    peer = iota((PEERS, NB), 0)
    takers = [v.astype(jnp.int32) >> 9 for v in leaves]
    parties = [owner[:, :NB], owner[:, NB:], *takers]
    shown = jnp.concatenate([jnp.where(peer == p, 1.0, 0.0) for p in parties], axis=0)
    count = running(shown)
    ranks = shown * (count - 1.0)
    rank_one, rank_two, *taker_rank = [
        jnp.sum(ranks[n * PEERS:(n + 1) * PEERS], axis=0, keepdims=True) for n in range(4)
    ]
    number_one, number_two, *number = [count[n * PEERS:(n + 1) * PEERS, NB - 1:] for n in range(4)]
    in_one = jnp.minimum(number_one, float(SOME))
    longest = [jnp.max(v, axis=0, keepdims=True) for v in number]
    peer = iota((PEERS, 1), 0)
    start_two = in_one + jnp.where(peer == 0, longest[0], jnp.where(peer == 1, longest[1], 0.0))
    start_two = jnp.maximum(start_two, jnp.maximum(CAP - number_two, float(CAP - SOME)))
    place_two = rank_two + jnp.sum(shown[PEERS:2 * PEERS] * start_two, axis=0, keepdims=True)
    place_one = jnp.where(rank_one < SOME, rank_one, rank_one + 2048.0)
    rank = jnp.concatenate([place_one, place_two], axis=1)
    most = jnp.max(rank)
    out_codes, in_codes = [], []
    for q in range(2):
        place = taker_rank[q] + in_one[q:q + 1]
        place = place.astype(jnp.int32)
        most = jnp.maximum(most, jnp.max(jnp.where(takers[q] < 0, 0, place).astype(F32)))
        out_codes.append(jnp.where(takers[q] >= 0, takers[q] * 4096 + place, -1))
        in_codes.append((place + (q * 4096 + 1)).astype(F32))
    most_ref[0] = most.astype(jnp.int32)
    mine = lane + (me * NB).astype(F32)
    out_rank = (down(column(source) == mine, column(rank) + 1.0) - 1.0).astype(jnp.int32)
    out_code = jnp.where(me == 0, out_codes[0], jnp.where(me == 1, out_codes[1], -1))
    hit = column(jnp.concatenate(leaves, axis=1)) == mine
    in_code = down(hit, column(jnp.concatenate(in_codes, axis=1))).astype(jnp.int32) - 1
    codes_ref[0:1] = out_rank
    codes_ref[1:2] = out_code
    codes_ref[2:8] = jnp.zeros((6, NB), jnp.int32)
    every_ref[:, :2 * NB] = owner * 4096 + rank.astype(jnp.int32)
    every_ref[:, 2 * NB:] = in_code
    parts = split2(panel_ref[...])
    for c in range(4):
        onehot = blocks_onehot(out_rank, out_code, 4 * c, 4)
        out_ref[4 * c * CAP:4 * (c + 1) * CAP] = pick_t(onehot, parts)


def make_plan(where, pivot_one, pivot_two, panel_t):
    return pl.pallas_call(
        plan_kernel,
        in_specs=[SMEM] + [VMEM] * 3,
        out_specs=[VMEM, VMEM, SMEM, VMEM],
        out_shape=[
            jax.ShapeDtypeStruct((8, NB), jnp.int32),
            jax.ShapeDtypeStruct((1, 3 * NB), jnp.int32),
            jax.ShapeDtypeStruct((1,), jnp.int32),
            jax.ShapeDtypeStruct((SLOTS, 128), F32),
        ],
        name="make_plan",
    )(where, pivot_one.reshape(1, NB), pivot_two.reshape(1, NB), panel_t)


def pack_kernel(codes_ref, rows_ref, out_ref, parts_ref):
    step = pl.program_id(0)

    @pl.when(step == 0)
    def _():
        for n, part in enumerate(split2(rows_ref[...])):
            parts_ref[n] = part

    onehot = blocks_onehot(codes_ref[0:1], codes_ref[1:2], step * 4, 4)
    out_ref[...] = pick(onehot, (parts_ref[0], parts_ref[1], parts_ref[2]))


def pack(codes, rows):
    width = rows.shape[1]
    return pl.pallas_call(
        pack_kernel,
        grid=(4,),
        in_specs=[pl.BlockSpec((8, NB), lambda i: (0, 0)), pl.BlockSpec((NB, width), lambda i: (0, 0))],
        out_specs=pl.BlockSpec((4 * CAP, width), lambda i: (i, 0)),
        out_shape=jax.ShapeDtypeStruct((SLOTS, width), F32),
        scratch_shapes=[pltpu.VMEM((3, NB, width), BF16)],
        name="pack_rows",
    )(codes, rows)


def slots_of(at_ref, n):
    code = at_ref[:, n * NB:(n + 1) * NB]
    place = code & 4095
    at = column(jnp.where(place < CAP, (code >> 12) * SOME + place - n * (CAP - SOME), -1))
    return jnp.where(iota((NB, FEW), 1) == at, 1.0, 0.0).astype(BF16)


def share(got, n):
    some = got[:, :SOME] if n == 0 else got[:, CAP - SOME:]
    return some.reshape(FEW, got.shape[2])


def arrivals(at_ref):
    code = at_ref[:, 2 * NB:]
    at = column(in_first(code))
    return jnp.where(iota((NB, 2 * CAP), 1) == at, 1.0, 0.0).astype(BF16), column(code) >= 0


def late(flag_ref, extra_ref, buffer, sem, target):
    @pl.when(flag_ref[0] >= CAP)
    def _():
        copy = pltpu.make_async_copy(extra_ref, buffer, sem)
        copy.start()
        copy.wait()

        def turn(n, carry):
            at = pl.ds(pl.multiple_of(n * 16, 16), 16)
            target[at] += buffer[at]
            return carry

        lax.fori_loop(0, target.shape[0] // 16, turn, 0)


def panel_rows_kernel(where_ref, flag_ref, at_ref, got_ref, extra_ref, keep_ref, send_ref, tops_ref, rows, more, sem):
    core = where_ref[1]
    got = got_ref[...]
    for n in range(2):
        rows[n * NB:(n + 1) * NB] = pick(slots_of(at_ref, n), split2(share(got, n)))
    late(flag_ref, extra_ref.at[:2 * NB, :128], more, sem, rows)
    first, second = rows[:NB], rows[NB:]
    left = iota((NB, 128), 1) < 64
    tops_ref[...] = jnp.where(left, first, second)
    swapped = jnp.where(left, second, first)
    upper = swapped[:HALF]
    lower = jnp.concatenate([swapped[HALF:], got[:2].reshape(2 * CAP, 128)], axis=0)
    keep_ref[...] = jnp.where(core == 0, upper, lower)
    send_ref[...] = jnp.where(core == 0, lower, upper)


def panel_rows(where, flag, at, got, extra):
    half = jax.ShapeDtypeStruct((HALF, 128), F32)
    return pl.pallas_call(
        panel_rows_kernel,
        in_specs=[SMEM] * 2 + [VMEM] * 2 + [ANY],
        out_specs=[VMEM] * 3,
        out_shape=[half, half, jax.ShapeDtypeStruct((NB, 128), F32)],
        scratch_shapes=[pltpu.VMEM((2 * NB, 128), F32), pltpu.VMEM((2 * NB, 128), F32), pltpu.SemaphoreType.DMA],
        name="panel_rows",
    )(where, flag, at, got, extra)


def fold_kernel(at_ref, lower_ref, one_ref, two_ref):
    for n, out in enumerate((one_ref, two_ref)):
        onehot = slots_of(at_ref, n)
        high, low = split2(lower_ref[n])
        out[0] = mm(high, onehot).astype(BF16)
        out[1] = mm(low, onehot).astype(BF16)


def fold(at, lower_inv):
    shape = jax.ShapeDtypeStruct((2, NB, FEW), BF16)
    return pl.pallas_call(
        fold_kernel, in_specs=[VMEM] * 2, out_specs=[VMEM] * 2, out_shape=[shape, shape], name="fold_slots"
    )(at, lower_inv)


def own_panels_kernel(where_ref, p0, p1, p2, p3, out_ref, gath):
    core, z = where_ref[1], where_ref[2]
    for s, piece in enumerate((p0, p1, p2, p3)):
        zz = lax.rem(z + 4 - s, 4)
        gath[zz, core] = piece[:128]
        gath[zz, 1 - core] = piece[128:]
    for n in range(2):
        half = [gath[c // 2, c % 2, 64 * n:64 * (n + 1)] for c in range(8)]
        out_ref[n] = jnp.transpose(jnp.concatenate(half, axis=0))


def own_panels(where, pieces):
    return pl.pallas_call(
        own_panels_kernel,
        in_specs=[SMEM] + [VMEM] * 4,
        out_specs=VMEM,
        out_shape=jax.ShapeDtypeStruct((2, NB, NB), F32),
        scratch_shapes=[pltpu.VMEM((4, 2, 128, NB), F32)],
        name="own_panels",
    )(where, *pieces)


def panel_math_kernel(where_ref, flag_ref, at_ref, tops_ref, whole_ref, extra_ref, k0, k1, k2, k3, p0, p1, p2, p3,
                      lower_ref, upper_ref, left_ref, pout_ref, gath, src, more, sem):
    me, core, z = where_ref[0], where_ref[1], where_ref[2]
    for s, (a, b) in enumerate(((k0, p0), (k1, p1), (k2, p2), (k3, p3))):
        zz = lax.rem(z + 4 - s, 4)
        gath[core, zz] = a[...]
        gath[1 - core, zz] = b[...]
    left = iota((2 * HALF, 128), 1) < 64
    ones, twos = [], []
    for zz in range(4):
        a = jnp.concatenate([gath[0, zz, :HALF], gath[1, zz, HALF:]], axis=0)
        b = jnp.concatenate([gath[0, zz, HALF:], gath[1, zz, :HALF]], axis=0)
        ones.append(jnp.where(left, a, pltpu.roll(b, 64, 1)))
        twos.append(jnp.where(left, pltpu.roll(a, 64, 1), b))
    in_one, in_two = jnp.concatenate(ones, axis=1), jnp.concatenate(twos, axis=1)
    onehot, moved = arrivals(at_ref)
    top_two_one, top_one_two = in_one[:NB], in_two[:NB]
    src[:NB] = jnp.where(moved, pick(onehot, split2(in_one[NB:])), whole_ref[0])
    src[NB:] = jnp.where(moved, pick(onehot, split2(in_two[NB:])), whole_ref[1])
    late(flag_ref, extra_ref, more, sem, src)
    own_one = jnp.where(me == 1, top_two_one, src[:NB])
    own_two = jnp.where(me == 1, 0.0, src[NB:])
    upper_one_inv = split2(upper_ref[0])
    lower_kept = dot3_upper(split2(own_one), upper_one_inv)
    lower_top = dot3_upper(split2(top_two_one), upper_one_inv)
    upper_panel = dot3_lower(split2(lower_ref[0]), split2(top_one_two))
    kept_parts = split2(lower_kept)
    updated = own_two - dot3(kept_parts, split2(upper_panel))
    lower_two = dot3_upper(split2(updated), split2(upper_ref[1]))
    left_ref[0], left_ref[1] = kept_parts
    left_ref[2], left_ref[3] = split2(lower_two)
    left_ref[4], left_ref[5] = split2(dot3_lower(split2(lower_ref[1]), split2(lower_top)))
    src[:NB] = lower_kept
    src[NB:] = jnp.where(me == 0, upper_panel, jnp.where(me == 1, updated, lower_two))
    at = pl.multiple_of(z * 128, 128)
    one = src[:NB, pl.ds(at, 128)]
    two = src[NB:, pl.ds(at, 128)]
    left = iota((NB, 128), 1) < 64
    mine = jnp.where(
        core == 0,
        jnp.where(left, one, pltpu.roll(two, 64, 1)),
        jnp.where(left, pltpu.roll(one, 64, 1), two),
    )
    tops = tops_ref[...]
    mine = jnp.where(left & (me == 0), tops, mine)
    mine = jnp.where(jnp.logical_not(left) & (me == 1), tops + mine, mine)
    pout_ref[...] = jnp.transpose(mine)


def panel_math(where, flag, at, tops, whole, extra, kept, other, lower_inv, upper_inv):
    return pl.pallas_call(
        panel_math_kernel,
        in_specs=[SMEM] * 2 + [VMEM] * 3 + [ANY] + [VMEM] * 10,
        out_specs=[VMEM] * 2,
        out_shape=[jax.ShapeDtypeStruct((6, NB, NB), BF16), jax.ShapeDtypeStruct((128, NB), F32)],
        scratch_shapes=[
            pltpu.VMEM((2, 4, 2 * HALF, 128), F32),
            pltpu.VMEM((2 * NB, NB), F32),
            pltpu.VMEM((2 * NB, NB), F32),
            pltpu.SemaphoreType.DMA,
        ],
        name="panel_math",
    )(where, flag, at, tops, whole, extra, *kept, *other, lower_inv, upper_inv)


WIDE = 256


def slab_kernel(where_ref, flag_ref, at_ref, got_ref, rows_ref, extra_ref, one_ref, two_ref, left_ref, out_ref,
                parts, more, sem):
    me = where_ref[0]
    at = pl.multiple_of(pl.program_id(0) * WIDE, WIDE)
    got = got_ref[...]
    onehot, moved = arrivals(at_ref)
    parts[2 * NB:] = jnp.where(moved, pick(onehot, split2(got[:2].reshape(2 * CAP, WIDE))), rows_ref[...])
    parts[:NB] = dot3((one_ref[0], one_ref[1]), split2(share(got, 0)))
    parts[NB:2 * NB] = dot3((two_ref[0], two_ref[1]), split2(share(got, 1)))

    late(flag_ref, extra_ref.at[:, pl.ds(at, WIDE)], more, sem, parts)
    upper_one = parts[:NB]
    one = split2(upper_one)
    upper_two = parts[NB:2 * NB] - dot3((left_ref[4], left_ref[5]), one)
    schur = parts[2 * NB:] - dot3((left_ref[0], left_ref[1]), one) - dot3((left_ref[2], left_ref[3]), split2(upper_two))
    out_ref[...] = jnp.where(me == 0, upper_one, jnp.where(me == 1, upper_two, schur))


def slab_math(where, flag, at, got, rows, extra, one, two, left):
    whole = lambda *shape: pl.BlockSpec(shape, lambda i: (0,) * len(shape))
    return pl.pallas_call(
        slab_kernel,
        grid=(NB // WIDE,),
        in_specs=[
            SMEM,
            SMEM,
            whole(1, 3 * NB),
            pl.BlockSpec((PEERS, CAP, WIDE), lambda i: (0, 0, i)),
            pl.BlockSpec((NB, WIDE), lambda i: (0, i)),
            ANY,
            whole(2, NB, FEW),
            whole(2, NB, FEW),
            whole(6, NB, NB),
        ],
        out_specs=pl.BlockSpec((NB, WIDE), lambda i: (0, i)),
        out_shape=jax.ShapeDtypeStruct((NB, NB), F32),
        scratch_shapes=[pltpu.VMEM((3 * NB, WIDE), F32), pltpu.VMEM((3 * NB, WIDE), F32), pltpu.SemaphoreType.DMA],
        name="slab_math",
    )(where, flag, at, got, rows, extra, one, two, left)


def mark_kernel(in_ref, out_ref):
    out_ref[0] = in_ref[0]


def mark(x):
    return pl.pallas_call(
        mark_kernel, in_specs=[SMEM], out_specs=SMEM, out_shape=jax.ShapeDtypeStruct((1,), jnp.int32), name="mark"
    )(x)


def exchange(blocks):
    width = blocks.shape[1]
    return lax.all_to_all(blocks.reshape(PEERS, CAP, width), RD, 0, 0)


def unused_kernel(*refs):
    pass


def unwritten(*shapes):
    return pl.pallas_call(
        unused_kernel,
        out_specs=[ANY] * len(shapes),
        out_shape=[jax.ShapeDtypeStruct(shape, F32) for shape in shapes],
        name="unwritten",
    )()


def late_pack_kernel(base_ref, codes_ref, panel_ref, rows_ref, out_ref):
    k = iota((CAP, NB), 0) + base_ref[0]
    picked = (k == codes_ref[0:1]) | ((k + pl.program_id(0) * 4096) == codes_ref[1:2])
    onehot = jnp.where(picked, 1.0, 0.0).astype(BF16)
    out_ref[:, :128] = pick_t(onehot, split2(panel_ref[...]))
    out_ref[:, 128:] = pick(onehot, split2(rows_ref[...]))


def late_pack(base, codes, panel_t, slab):
    whole = lambda *shape: pl.BlockSpec(shape, lambda i: (0,) * len(shape))
    return pl.pallas_call(
        late_pack_kernel,
        grid=(PEERS,),
        in_specs=[SMEM, whole(8, NB), whole(128, NB), whole(NB, NB)],
        out_specs=pl.BlockSpec((CAP, 128 + NB), lambda i: (i, 0)),
        out_shape=jax.ShapeDtypeStruct((SLOTS, 128 + NB), F32),
        name="late_pack",
    )(base, codes, panel_t, slab)


def late_place_kernel(base_ref, every_ref, got_ref, old_ref, out_ref):
    code = column(every_ref[...])
    place = (code & 4095) - base_ref[0]
    now = (code >= 0) & (place >= 0) & (place < CAP)
    at = jnp.where(now, (code >> 12) * CAP + place, -1)
    onehot = jnp.where(iota((128, SLOTS), 1) == at, 1.0, 0.0).astype(BF16)
    old = jnp.where(base_ref[0] == CAP, 0.0, old_ref[...])
    out_ref[...] = jnp.where(now, pick(onehot, split2(got_ref[...])), old)


def late_place(base, every, got, old):
    block = pl.BlockSpec((128, 128 + NB), lambda i: (i, 0))
    return pl.pallas_call(
        late_place_kernel,
        grid=(12,),
        in_specs=[
            SMEM,
            pl.BlockSpec((1, 128), lambda i: (0, i)),
            pl.BlockSpec((SLOTS, 128 + NB), lambda i: (0, 0)),
            block,
        ],
        out_specs=block,
        out_shape=jax.ShapeDtypeStruct((3 * NB, 128 + NB), F32),
        name="late_place",
    )(base, every, got, old)


def late_product_kernel(lower_ref, rows_ref, out_ref):
    n = pl.program_id(0)

    @pl.when(n < 8)
    def _():
        out_ref[...] = dot3(split2(lower_ref[0]), split2(rows_ref[:, 128:]))

    @pl.when(n >= 8)
    def _():
        at = pl.multiple_of(lax.rem(n, 4) * 128, 128)
        out_ref[...] = rows_ref[pl.ds(at, 128), 128:]


def late_product(lower_inv, rows):
    return pl.pallas_call(
        late_product_kernel,
        grid=(12,),
        in_specs=[
            pl.BlockSpec((1, 128, NB), lambda i: (lax.min(i // 4, 1), i % 4, 0)),
            pl.BlockSpec((NB, 128 + NB), lambda i: (i // 4, 0)),
        ],
        out_specs=pl.BlockSpec((128, NB), lambda i: (i, 0)),
        out_shape=jax.ShapeDtypeStruct((3 * NB, NB), F32),
        name="late_product",
    )(lower_inv, rows)


def late_panel_kernel(in_ref, out_ref):
    left = iota((NB, 128), 1) < 64
    a, b = in_ref[0], in_ref[1]
    out_ref[:NB] = jnp.where(left, a, pltpu.roll(b, 64, 1))
    out_ref[NB:] = jnp.where(left, pltpu.roll(a, 64, 1), b)


def late_panel(pieces):
    return pl.pallas_call(
        late_panel_kernel,
        grid=(4,),
        in_specs=[pl.BlockSpec((2, NB, 128), lambda i: (i, 0, 0))],
        out_specs=pl.BlockSpec((2 * NB, 128), lambda i: (0, i)),
        out_shape=jax.ShapeDtypeStruct((2 * NB, NB), F32),
        name="late_panel",
    )(pieces)


def late_exchange(blocks, me):
    ring = [(i, (i + 1) % PEERS) for i in range(PEERS)]

    def turn(t, state):
        held, got = state
        mine = lax.dynamic_slice_in_dim(held, me * CAP, CAP, 0)
        got = lax.dynamic_update_slice_in_dim(got, mine, (me - t) % PEERS * CAP, 0)
        return lax.ppermute(held, RD, ring), got

    return lax.fori_loop(0, PEERS, turn, (blocks, jnp.zeros(blocks.shape, F32)))[1]


def late_gather(rows, col):
    ring = [(i, (i + 1) % 8) for i in range(8)]

    def turn(t, state):
        held, got = state
        got = lax.dynamic_update_slice_in_dim(got, held[None], (col - t) % 8, 0)
        return lax.ppermute(held, "col", ring), got

    return lax.fori_loop(0, 8, turn, (rows, jnp.zeros((8, *rows.shape), F32)))[1]


def further_rounds(most, codes, every, panel_t, slab, lower_inv, me, col):
    def turn(state):
        r, rows = state[:2]
        base = (r * CAP).reshape(1)
        got = late_exchange(late_pack(base, codes, panel_t, slab), me)
        rows = late_place(base, every, got, rows)
        wide = late_panel(late_gather(rows[2 * NB:, :128], col))
        return r + 1, rows, wide, late_product(lower_inv, rows)

    start = (jnp.int32(1), *unwritten((3 * NB, 128 + NB), (2 * NB, NB), (3 * NB, NB)))
    return lax.while_loop(lambda s: s[0] * CAP <= most, turn, start)[1:]


def partner(x):
    return lax.ppermute(x, "col", [(c, c ^ 1) for c in range(8)])


def shift(x, by):
    return lax.ppermute(x, "col", [(c, (c // 2 + by) % 4 * 2 + c % 2) for c in range(8)])


def body(panels, slab, pivot_one, pivot_two, lower_inv, upper_inv):
    me = lax.axis_index(RD)
    col = lax.axis_index("col")
    where = jnp.stack([me, col % 2, col // 2, col]).astype(jnp.int32)
    panel_t = jnp.swapaxes(panels, 1, 2).reshape(128, NB)
    panel_pair = jnp.concatenate([panel_t, partner(panel_t)], axis=0)
    codes, every, most, blocks = make_plan(where, pivot_one, pivot_two, panel_t)
    got_panel = exchange(blocks)
    pieces = [panel_pair] + [shift(panel_pair, by) for by in (1, 2, 3)]
    whole = own_panels(where, pieces)
    blocks = pack(codes, slab)
    most = mark(most)
    late_rows, late_own, late_slab = further_rounds(most[0], codes, every, panel_t, slab, lower_inv, me, col)
    got_slab = exchange(blocks)
    keep, send, tops = panel_rows(where, most, every, got_panel, late_rows)
    pair = jnp.concatenate([keep, partner(send)], axis=0)
    shifted = [shift(pair, by) for by in (1, 2, 3)]
    one, two = fold(every, lower_inv)
    shifted, one, two = lax.optimization_barrier((shifted, one, two))
    kept = [pair] + shifted
    other = [partner(x) for x in kept]
    left, panel_out = panel_math(where, most, every, tops, whole, late_own, kept, other, lower_inv, upper_inv)
    slab_out = slab_math(where, most, every, got_slab, slab, late_slab, one, two, left)
    return jnp.swapaxes(panel_out.reshape(2, 64, NB), 1, 2), slab_out


def solution(mesh):
    placed = (P(None, RD, "col"), P(RD, "col"), P(), P(), P(), P())
    return jax.shard_map(
        body,
        mesh=mesh,
        in_specs=placed,
        out_specs=(P(None, RD, "col"), P(RD, "col")),
        check_vma=False,
    )
```

```python
import jax
import jax.numpy as jnp
from jax import lax
from jax.experimental import pallas as pl
from jax.experimental.pallas import tpu as pltpu
from jax.sharding import PartitionSpec as P


NB = 512
CAP = 96
PEERS = 16
SLOTS = PEERS * CAP
SOME = 64
FEW = PEERS * SOME
HALF = (NB + 2 * CAP) // 2
RD = ("row", "depth")
F32 = jnp.float32
BF16 = jnp.bfloat16
GRANT = 24 * 2**20
VMEM = pl.BlockSpec(memory_space=pltpu.VMEM)
ANY = pl.BlockSpec(memory_space=pl.ANY)
SMEM = pl.BlockSpec(memory_space=pltpu.SMEM)


def iota(shape, axis):
    return lax.broadcasted_iota(jnp.int32, shape, axis)


def split2(x):
    high = x.astype(BF16)
    return high, (x - high.astype(F32)).astype(BF16)


def mm(a, b):
    return jnp.dot(a, b, preferred_element_type=F32)


def dot3(a, b):
    both = jnp.concatenate([a[0], a[1]], axis=1)
    return mm(both, jnp.concatenate([b[0], b[0]], axis=0)) + mm(a[0], b[1])


def cut(parts, rows, cols):
    return tuple(p[rows, cols] for p in parts)


FIRST, LAST, ALL = slice(0, NB // 2), slice(NB // 2, NB), slice(None)


def dot3_upper(a, b):
    left = dot3(cut(a, ALL, FIRST), cut(b, FIRST, FIRST))
    return jnp.concatenate([left, dot3(a, cut(b, ALL, LAST))], axis=1)


def dot3_lower(a, b):
    top = dot3(cut(a, FIRST, FIRST), cut(b, FIRST, ALL))
    return jnp.concatenate([top, dot3(cut(a, LAST, ALL), b)], axis=0)


def pick(onehot, parts):
    width = parts[0].shape[1]
    if width > 128:
        return mm(onehot, parts[0]) + mm(onehot, parts[1])
    both = mm(onehot, jnp.concatenate(parts, axis=1))
    return both[:, :width] + both[:, width:]


def pick_t(onehot, parts):
    both = jnp.concatenate(parts, axis=0)
    both = lax.dot_general(onehot, both, (((1,), (1,)), ((), ())), preferred_element_type=F32)
    return both[:, :128] + both[:, 128:]


def in_first(code):
    return jnp.where((code & 4095) < CAP, (code >> 12) * CAP + (code & 4095), -1)


def column(row):
    return jnp.transpose(jnp.broadcast_to(row, (8, row.shape[1])))[:, :1]


def running(x):
    n = x.shape[1]
    upto = jnp.where(iota((n, n), 0) <= iota((n, n), 1), 1.0, 0.0).astype(BF16)
    return mm(x.astype(BF16), upto)


def down(mask, value):
    return jnp.sum(jnp.where(mask, value, 0.0), axis=0, keepdims=True)


def blocks_onehot(rank, code, first, count):
    k = iota((CAP, NB), 0)
    held = k == rank
    code = in_first(code)
    blocks = [
        jnp.where(held | ((k + (first + b) * CAP) == code), 1.0, 0.0).astype(BF16) for b in range(count)
    ]
    return jnp.concatenate(blocks, axis=0)


def plan_kernel(where_ref, one_ref, two_ref, panel_ref, codes_ref, every_ref, most_ref, out_ref):
    me = where_ref[0]
    one, two = one_ref[...].astype(F32), two_ref[...].astype(F32)
    one_c, two_c = column(one), column(two)
    lane = iota((1, NB), 1).astype(F32)
    sub = iota((NB, 1), 0).astype(F32)
    hit = down(one_c == two, sub + 1.0)
    source = jnp.concatenate([one, jnp.where(hit > 0, hit - 1.0, two)], axis=1)
    again = down(two_c == one, 1.0) > 0
    taken = down(one_c == lane + NB, 1.0) > 0
    onward = down(sub + NB == one, two_c)
    leaves = (
        jnp.where(again, -1.0, jnp.where(one < 2 * NB, onward, one)),
        jnp.where(taken, -1.0, two),
    )
    owner = source.astype(jnp.int32) >> 9
    peer = iota((PEERS, NB), 0)
    takers = [v.astype(jnp.int32) >> 9 for v in leaves]
    parties = [owner[:, :NB], owner[:, NB:], *takers]
    shown = jnp.concatenate([jnp.where(peer == p, 1.0, 0.0) for p in parties], axis=0)
    count = running(shown)
    ranks = shown * (count - 1.0)
    rank_one, rank_two, *taker_rank = [
        jnp.sum(ranks[n * PEERS:(n + 1) * PEERS], axis=0, keepdims=True) for n in range(4)
    ]
    number_one, number_two, *number = [count[n * PEERS:(n + 1) * PEERS, NB - 1:] for n in range(4)]
    in_one = jnp.minimum(number_one, float(SOME))
    longest = [jnp.max(v, axis=0, keepdims=True) for v in number]
    peer = iota((PEERS, 1), 0)
    start_two = in_one + jnp.where(peer == 0, longest[0], jnp.where(peer == 1, longest[1], 0.0))
    start_two = jnp.maximum(start_two, jnp.maximum(CAP - number_two, float(CAP - SOME)))
    place_two = rank_two + jnp.sum(shown[PEERS:2 * PEERS] * start_two, axis=0, keepdims=True)
    place_one = jnp.where(rank_one < SOME, rank_one, rank_one + 2048.0)
    rank = jnp.concatenate([place_one, place_two], axis=1)
    most = jnp.max(rank)
    out_codes, in_codes = [], []
    for q in range(2):
        place = taker_rank[q] + in_one[q:q + 1]
        place = place.astype(jnp.int32)
        most = jnp.maximum(most, jnp.max(jnp.where(takers[q] < 0, 0, place).astype(F32)))
        out_codes.append(jnp.where(takers[q] >= 0, takers[q] * 4096 + place, -1))
        in_codes.append((place + (q * 4096 + 1)).astype(F32))
    most_ref[0] = most.astype(jnp.int32)
    mine = lane + (me * NB).astype(F32)
    out_rank = (down(column(source) == mine, column(rank) + 1.0) - 1.0).astype(jnp.int32)
    out_code = jnp.where(me == 0, out_codes[0], jnp.where(me == 1, out_codes[1], -1))
    hit = column(jnp.concatenate(leaves, axis=1)) == mine
    in_code = down(hit, column(jnp.concatenate(in_codes, axis=1))).astype(jnp.int32) - 1
    codes_ref[0:1] = out_rank
    codes_ref[1:2] = out_code
    codes_ref[2:8] = jnp.zeros((6, NB), jnp.int32)
    every_ref[:, :2 * NB] = owner * 4096 + rank.astype(jnp.int32)
    every_ref[:, 2 * NB:] = in_code
    parts = split2(panel_ref[...])
    for c in range(4):
        onehot = blocks_onehot(out_rank, out_code, 4 * c, 4)
        out_ref[4 * c * CAP:4 * (c + 1) * CAP] = pick_t(onehot, parts)


def make_plan(where, pivot_one, pivot_two, panel_t):
    return pl.pallas_call(
        plan_kernel,
        in_specs=[SMEM] + [VMEM] * 3,
        out_specs=[VMEM, VMEM, SMEM, VMEM],
        out_shape=[
            jax.ShapeDtypeStruct((8, NB), jnp.int32),
            jax.ShapeDtypeStruct((1, 3 * NB), jnp.int32),
            jax.ShapeDtypeStruct((1,), jnp.int32),
            jax.ShapeDtypeStruct((SLOTS, 128), F32),
        ],
        name="make_plan",
    )(where, pivot_one.reshape(1, NB), pivot_two.reshape(1, NB), panel_t)


def pack_kernel(codes_ref, rows_ref, out_ref, parts_ref):
    step = pl.program_id(0)

    @pl.when(step == 0)
    def _():
        for n, part in enumerate(split2(rows_ref[...])):
            parts_ref[n] = part

    onehot = blocks_onehot(codes_ref[0:1], codes_ref[1:2], step * 4, 4)
    out_ref[...] = pick(onehot, (parts_ref[0], parts_ref[1], parts_ref[2]))


def pack(codes, rows):
    width = rows.shape[1]
    return pl.pallas_call(
        pack_kernel,
        grid=(4,),
        in_specs=[pl.BlockSpec((8, NB), lambda i: (0, 0)), pl.BlockSpec((NB, width), lambda i: (0, 0))],
        out_specs=pl.BlockSpec((4 * CAP, width), lambda i: (i, 0)),
        out_shape=jax.ShapeDtypeStruct((SLOTS, width), F32),
        scratch_shapes=[pltpu.VMEM((3, NB, width), BF16)],
        name="pack_rows",
    )(codes, rows)


def slots_of(at_ref, n):
    code = at_ref[:, n * NB:(n + 1) * NB]
    place = code & 4095
    at = column(jnp.where(place < CAP, (code >> 12) * SOME + place - n * (CAP - SOME), -1))
    return jnp.where(iota((NB, FEW), 1) == at, 1.0, 0.0).astype(BF16)


def share(got, n):
    some = got[:, :SOME] if n == 0 else got[:, CAP - SOME:]
    return some.reshape(FEW, got.shape[2])


def arrivals(at_ref):
    code = at_ref[:, 2 * NB:]
    at = column(in_first(code))
    return jnp.where(iota((NB, 2 * CAP), 1) == at, 1.0, 0.0).astype(BF16), column(code) >= 0


def late(flag_ref, extra_ref, buffer, sem, first=True):
    @pl.when((flag_ref[0] < CAP) & first)
    def _():
        buffer[...] = jnp.zeros_like(buffer)

    @pl.when(flag_ref[0] >= CAP)
    def _():
        copy = pltpu.make_async_copy(extra_ref, buffer, sem)
        copy.start()
        copy.wait()

    return buffer


def panel_rows_kernel(where_ref, flag_ref, at_ref, got_ref, extra_ref, keep_ref, send_ref, tops_ref, more, sem):
    core = where_ref[1]
    more = late(flag_ref, extra_ref.at[:2 * NB, :128], more, sem)
    got = got_ref[...]
    first = pick(slots_of(at_ref, 0), split2(share(got, 0))) + more[:NB]
    second = pick(slots_of(at_ref, 1), split2(share(got, 1))) + more[NB:]
    left = iota((NB, 128), 1) < 64
    tops_ref[...] = jnp.where(left, first, second)
    swapped = jnp.where(left, second, first)
    upper = swapped[:HALF]
    lower = jnp.concatenate([swapped[HALF:], got[:2].reshape(2 * CAP, 128)], axis=0)
    keep_ref[...] = jnp.where(core == 0, upper, lower)
    send_ref[...] = jnp.where(core == 0, lower, upper)


def panel_rows(where, flag, at, got, extra):
    half = jax.ShapeDtypeStruct((HALF, 128), F32)
    return pl.pallas_call(
        panel_rows_kernel,
        in_specs=[SMEM] * 2 + [VMEM] * 2 + [ANY],
        out_specs=[VMEM] * 3,
        out_shape=[half, half, jax.ShapeDtypeStruct((NB, 128), F32)],
        scratch_shapes=[pltpu.VMEM((2 * NB, 128), F32), pltpu.SemaphoreType.DMA],
        compiler_params=pltpu.CompilerParams(vmem_limit_bytes=GRANT),
        name="panel_rows",
    )(where, flag, at, got, extra)


def fold_kernel(at_ref, lower_ref, one_ref, two_ref):
    for n, out in enumerate((one_ref, two_ref)):
        onehot = slots_of(at_ref, n)
        high, low = split2(lower_ref[n])
        out[0] = mm(high, onehot).astype(BF16)
        out[1] = mm(low, onehot).astype(BF16)


def fold(at, lower_inv):
    shape = jax.ShapeDtypeStruct((2, NB, FEW), BF16)
    return pl.pallas_call(
        fold_kernel, in_specs=[VMEM] * 2, out_specs=[VMEM] * 2, out_shape=[shape, shape], name="fold_slots"
    )(at, lower_inv)


def own_panels_kernel(where_ref, p0, p1, p2, p3, out_ref, gath):
    core, z = where_ref[1], where_ref[2]
    for s, piece in enumerate((p0, p1, p2, p3)):
        zz = lax.rem(z + 4 - s, 4)
        gath[zz, core] = piece[:128]
        gath[zz, 1 - core] = piece[128:]
    for n in range(2):
        half = [gath[c // 2, c % 2, 64 * n:64 * (n + 1)] for c in range(8)]
        out_ref[n] = jnp.transpose(jnp.concatenate(half, axis=0))


def own_panels(where, pieces):
    return pl.pallas_call(
        own_panels_kernel,
        in_specs=[SMEM] + [VMEM] * 4,
        out_specs=VMEM,
        out_shape=jax.ShapeDtypeStruct((2, NB, NB), F32),
        scratch_shapes=[pltpu.VMEM((4, 2, 128, NB), F32)],
        compiler_params=pltpu.CompilerParams(vmem_limit_bytes=GRANT),
        name="own_panels",
    )(where, *pieces)


def panel_math_kernel(where_ref, flag_ref, at_ref, tops_ref, whole_ref, extra_ref, k0, k1, k2, k3, p0, p1, p2, p3,
                      lower_ref, upper_ref, left_ref, pout_ref, gath, src, more, sem):
    me, core, z = where_ref[0], where_ref[1], where_ref[2]
    for s, (a, b) in enumerate(((k0, p0), (k1, p1), (k2, p2), (k3, p3))):
        zz = lax.rem(z + 4 - s, 4)
        gath[core, zz] = a[...]
        gath[1 - core, zz] = b[...]
    more = late(flag_ref, extra_ref, more, sem)
    left = iota((2 * HALF, 128), 1) < 64
    ones, twos = [], []
    for zz in range(4):
        a = jnp.concatenate([gath[0, zz, :HALF], gath[1, zz, HALF:]], axis=0)
        b = jnp.concatenate([gath[0, zz, HALF:], gath[1, zz, :HALF]], axis=0)
        ones.append(jnp.where(left, a, pltpu.roll(b, 64, 1)))
        twos.append(jnp.where(left, pltpu.roll(a, 64, 1), b))
    in_one, in_two = jnp.concatenate(ones, axis=1), jnp.concatenate(twos, axis=1)
    onehot, moved = arrivals(at_ref)
    top_two_one, top_one_two = in_one[:NB], in_two[:NB]
    own_one = jnp.where(moved, pick(onehot, split2(in_one[NB:])) + more[0], whole_ref[0])
    own_two = jnp.where(moved, pick(onehot, split2(in_two[NB:])) + more[1], whole_ref[1])
    own_one = jnp.where(me == 1, top_two_one, own_one)
    own_two = jnp.where(me == 1, 0.0, own_two)
    upper_one_inv = split2(upper_ref[0])
    lower_kept = dot3_upper(split2(own_one), upper_one_inv)
    lower_top = dot3_upper(split2(top_two_one), upper_one_inv)
    upper_panel = dot3_lower(split2(lower_ref[0]), split2(top_one_two))
    kept_parts = split2(lower_kept)
    updated = own_two - dot3(kept_parts, split2(upper_panel))
    lower_two = dot3_upper(split2(updated), split2(upper_ref[1]))
    left_ref[0], left_ref[1] = kept_parts
    left_ref[2], left_ref[3] = split2(lower_two)
    left_ref[4], left_ref[5] = split2(dot3_lower(split2(lower_ref[1]), split2(lower_top)))
    src[0] = lower_kept
    src[1] = jnp.where(me == 0, upper_panel, jnp.where(me == 1, updated, lower_two))
    at = pl.multiple_of(z * 128, 128)
    one = src[0, :, pl.ds(at, 128)]
    two = src[1, :, pl.ds(at, 128)]
    left = iota((NB, 128), 1) < 64
    mine = jnp.where(
        core == 0,
        jnp.where(left, one, pltpu.roll(two, 64, 1)),
        jnp.where(left, pltpu.roll(one, 64, 1), two),
    )
    tops = tops_ref[...]
    mine = jnp.where(left & (me == 0), tops, mine)
    mine = jnp.where(jnp.logical_not(left) & (me == 1), tops + mine, mine)
    pout_ref[...] = jnp.transpose(mine)


def panel_math(where, flag, at, tops, whole, extra, kept, other, lower_inv, upper_inv):
    return pl.pallas_call(
        panel_math_kernel,
        in_specs=[SMEM] * 2 + [VMEM] * 3 + [ANY] + [VMEM] * 10,
        out_specs=[VMEM] * 2,
        out_shape=[jax.ShapeDtypeStruct((6, NB, NB), BF16), jax.ShapeDtypeStruct((128, NB), F32)],
        scratch_shapes=[
            pltpu.VMEM((2, 4, 2 * HALF, 128), F32),
            pltpu.VMEM((2, NB, NB), F32),
            pltpu.VMEM((2, NB, NB), F32),
            pltpu.SemaphoreType.DMA,
        ],
        compiler_params=pltpu.CompilerParams(vmem_limit_bytes=GRANT),
        name="panel_math",
    )(where, flag, at, tops, whole, extra, *kept, *other, lower_inv, upper_inv)


WIDE = 256


def slab_kernel(where_ref, flag_ref, at_ref, got_ref, rows_ref, extra_ref, one_ref, two_ref, left_ref, out_ref,
                more, sem):
    me = where_ref[0]
    at = pl.multiple_of(pl.program_id(0) * WIDE, WIDE)
    more = late(flag_ref, extra_ref.at[:, pl.ds(at, WIDE)], more, sem, pl.program_id(0) == 0)
    got = got_ref[...]
    upper_one = dot3((one_ref[0], one_ref[1]), split2(share(got, 0))) + more[:NB]
    one = split2(upper_one)
    upper_two = (dot3((two_ref[0], two_ref[1]), split2(share(got, 1))) - dot3((left_ref[4], left_ref[5]), one)) + more[NB:2 * NB]

    @pl.when(me == 0)
    def _():
        out_ref[...] = upper_one

    @pl.when(me == 1)
    def _():
        out_ref[...] = upper_two

    @pl.when(me > 1)
    def _():
        onehot, moved = arrivals(at_ref)
        own = jnp.where(moved, pick(onehot, split2(got[:2].reshape(2 * CAP, WIDE))) + more[2 * NB:], rows_ref[...])
        two = split2(upper_two)
        out_ref[...] = own - dot3((left_ref[0], left_ref[1]), one) - dot3((left_ref[2], left_ref[3]), two)


def slab_math(where, flag, at, got, rows, extra, one, two, left):
    whole = lambda *shape: pl.BlockSpec(shape, lambda i: (0,) * len(shape))
    return pl.pallas_call(
        slab_kernel,
        grid=(NB // WIDE,),
        in_specs=[
            SMEM,
            SMEM,
            whole(1, 3 * NB),
            pl.BlockSpec((PEERS, CAP, WIDE), lambda i: (0, 0, i)),
            pl.BlockSpec((NB, WIDE), lambda i: (0, i)),
            ANY,
            whole(2, NB, FEW),
            whole(2, NB, FEW),
            whole(6, NB, NB),
        ],
        out_specs=pl.BlockSpec((NB, WIDE), lambda i: (0, i)),
        out_shape=jax.ShapeDtypeStruct((NB, NB), F32),
        scratch_shapes=[pltpu.VMEM((3 * NB, WIDE), F32), pltpu.SemaphoreType.DMA],
        name="slab_math",
    )(where, flag, at, got, rows, extra, one, two, left)


def mark_kernel(in_ref, out_ref):
    out_ref[0] = in_ref[0]


def mark(x):
    return pl.pallas_call(
        mark_kernel, in_specs=[SMEM], out_specs=SMEM, out_shape=jax.ShapeDtypeStruct((1,), jnp.int32), name="mark"
    )(x)


def exchange(blocks):
    width = blocks.shape[1]
    return lax.all_to_all(blocks.reshape(PEERS, CAP, width), RD, 0, 0)


def unused_kernel(*refs):
    pass


def unwritten(*shapes):
    return pl.pallas_call(
        unused_kernel,
        out_specs=[ANY] * len(shapes),
        out_shape=[jax.ShapeDtypeStruct(shape, F32) for shape in shapes],
        name="unwritten",
    )()


def late_pack_kernel(base_ref, codes_ref, panel_ref, rows_ref, out_ref):
    k = iota((CAP, NB), 0) + base_ref[0]
    picked = (k == codes_ref[0:1]) | ((k + pl.program_id(0) * 4096) == codes_ref[1:2])
    onehot = jnp.where(picked, 1.0, 0.0).astype(BF16)
    out_ref[:, :128] = pick_t(onehot, split2(panel_ref[...]))
    out_ref[:, 128:] = pick(onehot, split2(rows_ref[...]))


def late_pack(base, codes, panel_t, slab):
    whole = lambda *shape: pl.BlockSpec(shape, lambda i: (0,) * len(shape))
    return pl.pallas_call(
        late_pack_kernel,
        grid=(PEERS,),
        in_specs=[SMEM, whole(8, NB), whole(128, NB), whole(NB, NB)],
        out_specs=pl.BlockSpec((CAP, 128 + NB), lambda i: (i, 0)),
        out_shape=jax.ShapeDtypeStruct((SLOTS, 128 + NB), F32),
        name="late_pack",
    )(base, codes, panel_t, slab)


def late_place_kernel(base_ref, every_ref, got_ref, old_ref, out_ref):
    code = column(every_ref[...])
    place = (code & 4095) - base_ref[0]
    now = (code >= 0) & (place >= 0) & (place < CAP)
    at = jnp.where(now, (code >> 12) * CAP + place, -1)
    onehot = jnp.where(iota((128, SLOTS), 1) == at, 1.0, 0.0).astype(BF16)
    old = jnp.where(base_ref[0] == CAP, 0.0, old_ref[...])
    out_ref[...] = jnp.where(now, pick(onehot, split2(got_ref[...])), old)


def late_place(base, every, got, old):
    block = pl.BlockSpec((128, 128 + NB), lambda i: (i, 0))
    return pl.pallas_call(
        late_place_kernel,
        grid=(12,),
        in_specs=[
            SMEM,
            pl.BlockSpec((1, 128), lambda i: (0, i)),
            pl.BlockSpec((SLOTS, 128 + NB), lambda i: (0, 0)),
            block,
        ],
        out_specs=block,
        out_shape=jax.ShapeDtypeStruct((3 * NB, 128 + NB), F32),
        name="late_place",
    )(base, every, got, old)


def late_product_kernel(lower_ref, rows_ref, out_ref):
    n = pl.program_id(0)

    @pl.when(n < 8)
    def _():
        out_ref[...] = dot3(split2(lower_ref[0]), split2(rows_ref[:, 128:]))

    @pl.when(n >= 8)
    def _():
        at = pl.multiple_of(lax.rem(n, 4) * 128, 128)
        out_ref[...] = rows_ref[pl.ds(at, 128), 128:]


def late_product(lower_inv, rows):
    return pl.pallas_call(
        late_product_kernel,
        grid=(12,),
        in_specs=[
            pl.BlockSpec((1, 128, NB), lambda i: (lax.min(i // 4, 1), i % 4, 0)),
            pl.BlockSpec((NB, 128 + NB), lambda i: (i // 4, 0)),
        ],
        out_specs=pl.BlockSpec((128, NB), lambda i: (i, 0)),
        out_shape=jax.ShapeDtypeStruct((3 * NB, NB), F32),
        name="late_product",
    )(lower_inv, rows)


def late_panel_kernel(in_ref, out_ref):
    left = iota((NB, 128), 1) < 64
    a, b = in_ref[0], in_ref[1]
    out_ref[0] = jnp.where(left, a, pltpu.roll(b, 64, 1))
    out_ref[1] = jnp.where(left, pltpu.roll(a, 64, 1), b)


def late_panel(pieces):
    return pl.pallas_call(
        late_panel_kernel,
        grid=(4,),
        in_specs=[pl.BlockSpec((2, NB, 128), lambda i: (i, 0, 0))],
        out_specs=pl.BlockSpec((2, NB, 128), lambda i: (0, 0, i)),
        out_shape=jax.ShapeDtypeStruct((2, NB, NB), F32),
        name="late_panel",
    )(pieces)


def late_exchange(blocks, me):
    ring = [(i, (i + 1) % PEERS) for i in range(PEERS)]

    def turn(t, state):
        held, got = state
        mine = lax.dynamic_slice_in_dim(held, me * CAP, CAP, 0)
        got = lax.dynamic_update_slice_in_dim(got, mine, (me - t) % PEERS * CAP, 0)
        return lax.ppermute(held, RD, ring), got

    return lax.fori_loop(0, PEERS, turn, (blocks, jnp.zeros(blocks.shape, F32)))[1]


def late_gather(rows, col):
    ring = [(i, (i + 1) % 8) for i in range(8)]

    def turn(t, state):
        held, got = state
        got = lax.dynamic_update_slice_in_dim(got, held[None], (col - t) % 8, 0)
        return lax.ppermute(held, "col", ring), got

    return lax.fori_loop(0, 8, turn, (rows, jnp.zeros((8, *rows.shape), F32)))[1]


def further_rounds(most, codes, every, panel_t, slab, lower_inv, me, col):
    def turn(state):
        r, rows = state[:2]
        base = (r * CAP).reshape(1)
        got = late_exchange(late_pack(base, codes, panel_t, slab), me)
        rows = late_place(base, every, got, rows)
        wide = late_panel(late_gather(rows[2 * NB:, :128], col))
        return r + 1, rows, wide, late_product(lower_inv, rows)

    start = (jnp.int32(1), *unwritten((3 * NB, 128 + NB), (2, NB, NB), (3 * NB, NB)))
    return lax.while_loop(lambda s: s[0] * CAP <= most, turn, start)[1:]


def partner(x):
    return lax.ppermute(x, "col", [(c, c ^ 1) for c in range(8)])


def shift(x, by):
    return lax.ppermute(x, "col", [(c, (c // 2 + by) % 4 * 2 + c % 2) for c in range(8)])


def body(panels, slab, pivot_one, pivot_two, lower_inv, upper_inv):
    me = lax.axis_index(RD)
    col = lax.axis_index("col")
    where = jnp.stack([me, col % 2, col // 2, col]).astype(jnp.int32)
    panel_t = jnp.swapaxes(panels, 1, 2).reshape(128, NB)
    panel_pair = jnp.concatenate([panel_t, partner(panel_t)], axis=0)
    codes, every, most, blocks = make_plan(where, pivot_one, pivot_two, panel_t)
    got_panel = exchange(blocks)
    pieces = [panel_pair] + [shift(panel_pair, by) for by in (1, 2, 3)]
    whole = own_panels(where, pieces)
    blocks = pack(codes, slab)
    most = mark(most)
    late_rows, late_own, late_slab = further_rounds(most[0], codes, every, panel_t, slab, lower_inv, me, col)
    got_slab = exchange(blocks)
    keep, send, tops = panel_rows(where, most, every, got_panel, late_rows)
    pair = jnp.concatenate([keep, partner(send)], axis=0)
    shifted = [shift(pair, by) for by in (1, 2, 3)]
    one, two = fold(every, lower_inv)
    shifted, one, two = lax.optimization_barrier((shifted, one, two))
    kept = [pair] + shifted
    other = [partner(x) for x in kept]
    left, panel_out = panel_math(where, most, every, tops, whole, late_own, kept, other, lower_inv, upper_inv)
    slab_out = slab_math(where, most, every, got_slab, slab, late_slab, one, two, left)
    return jnp.swapaxes(panel_out.reshape(2, 64, NB), 1, 2), slab_out


def solution(mesh):
    placed = (P(None, RD, "col"), P(RD, "col"), P(), P(), P(), P())
    return jax.shard_map(
        body,
        mesh=mesh,
        in_specs=placed,
        out_specs=(P(None, RD, "col"), P(RD, "col")),
        check_vma=False,
    )
```

```python
import jax
import jax.numpy as jnp
from jax import lax
from jax.experimental import pallas as pl
from jax.experimental.pallas import tpu as pltpu
from jax.sharding import PartitionSpec as P


NB = 512
CAP = 96
PEERS = 16
SLOTS = PEERS * CAP
SOME = 64
FEW = PEERS * SOME
HALF = (NB + 2 * CAP) // 2
RD = ("row", "depth")
F32 = jnp.float32
BF16 = jnp.bfloat16
GRANT = 24 * 2**20
VMEM = pl.BlockSpec(memory_space=pltpu.VMEM)
ANY = pl.BlockSpec(memory_space=pl.ANY)
SMEM = pl.BlockSpec(memory_space=pltpu.SMEM)


def iota(shape, axis):
    return lax.broadcasted_iota(jnp.int32, shape, axis)


def split2(x):
    high = x.astype(BF16)
    return high, (x - high.astype(F32)).astype(BF16)


def mm(a, b):
    return jnp.dot(a, b, preferred_element_type=F32)


def dot3(a, b):
    both = jnp.concatenate([a[0], a[1]], axis=1)
    return mm(both, jnp.concatenate([b[0], b[0]], axis=0)) + mm(a[0], b[1])


def cut(parts, rows, cols):
    return tuple(p[rows, cols] for p in parts)


FIRST, LAST, ALL = slice(0, NB // 2), slice(NB // 2, NB), slice(None)


def dot3_upper(a, b):
    left = dot3(cut(a, ALL, FIRST), cut(b, FIRST, FIRST))
    return jnp.concatenate([left, dot3(a, cut(b, ALL, LAST))], axis=1)


def dot3_lower(a, b):
    top = dot3(cut(a, FIRST, FIRST), cut(b, FIRST, ALL))
    return jnp.concatenate([top, dot3(cut(a, LAST, ALL), b)], axis=0)


def pick(onehot, parts):
    width = parts[0].shape[1]
    if width > 128:
        return mm(onehot, parts[0]) + mm(onehot, parts[1])
    both = mm(onehot, jnp.concatenate(parts, axis=1))
    return both[:, :width] + both[:, width:]


def pick_t(onehot, parts):
    both = jnp.concatenate(parts, axis=0)
    both = lax.dot_general(onehot, both, (((1,), (1,)), ((), ())), preferred_element_type=F32)
    return both[:, :128] + both[:, 128:]


def in_first(code):
    return jnp.where((code & 4095) < CAP, (code >> 12) * CAP + (code & 4095), -1)


def column(row):
    return jnp.transpose(jnp.broadcast_to(row, (8, row.shape[1])))[:, :1]


def running(x):
    n = x.shape[1]
    upto = jnp.where(iota((n, n), 0) <= iota((n, n), 1), 1.0, 0.0).astype(BF16)
    return mm(x.astype(BF16), upto)


def down(mask, value):
    return jnp.sum(jnp.where(mask, value, 0.0), axis=0, keepdims=True)


def blocks_onehot(rank, code, first, count):
    k = iota((CAP, NB), 0)
    held = k == rank
    code = in_first(code)
    blocks = [
        jnp.where(held | ((k + (first + b) * CAP) == code), 1.0, 0.0).astype(BF16) for b in range(count)
    ]
    return jnp.concatenate(blocks, axis=0)


def plan_kernel(where_ref, one_ref, two_ref, panel_ref, codes_ref, every_ref, most_ref, out_ref):
    me = where_ref[0]
    one, two = one_ref[...].astype(F32), two_ref[...].astype(F32)
    one_c, two_c = column(one), column(two)
    lane = iota((1, NB), 1).astype(F32)
    sub = iota((NB, 1), 0).astype(F32)
    hit = down(one_c == two, sub + 1.0)
    source = jnp.concatenate([one, jnp.where(hit > 0, hit - 1.0, two)], axis=1)
    again = down(two_c == one, 1.0) > 0
    taken = down(one_c == lane + NB, 1.0) > 0
    onward = down(sub + NB == one, two_c)
    leaves = (
        jnp.where(again, -1.0, jnp.where(one < 2 * NB, onward, one)),
        jnp.where(taken, -1.0, two),
    )
    owner = source.astype(jnp.int32) >> 9
    peer = iota((PEERS, NB), 0)
    takers = [v.astype(jnp.int32) >> 9 for v in leaves]
    parties = [owner[:, :NB], owner[:, NB:], *takers]
    shown = jnp.concatenate([jnp.where(peer == p, 1.0, 0.0) for p in parties], axis=0)
    count = running(shown)
    ranks = shown * (count - 1.0)
    rank_one, rank_two, *taker_rank = [
        jnp.sum(ranks[n * PEERS:(n + 1) * PEERS], axis=0, keepdims=True) for n in range(4)
    ]
    number_one, number_two, *number = [count[n * PEERS:(n + 1) * PEERS, NB - 1:] for n in range(4)]
    in_one = jnp.minimum(number_one, float(SOME))
    longest = [jnp.max(v, axis=0, keepdims=True) for v in number]
    peer = iota((PEERS, 1), 0)
    start_two = in_one + jnp.where(peer == 0, longest[0], jnp.where(peer == 1, longest[1], 0.0))
    start_two = jnp.maximum(start_two, jnp.maximum(CAP - number_two, float(CAP - SOME)))
    place_two = rank_two + jnp.sum(shown[PEERS:2 * PEERS] * start_two, axis=0, keepdims=True)
    place_one = jnp.where(rank_one < SOME, rank_one, rank_one + 2048.0)
    rank = jnp.concatenate([place_one, place_two], axis=1)
    most = jnp.max(rank)
    out_codes, in_codes = [], []
    for q in range(2):
        place = taker_rank[q] + in_one[q:q + 1]
        place = place.astype(jnp.int32)
        most = jnp.maximum(most, jnp.max(jnp.where(takers[q] < 0, 0, place).astype(F32)))
        out_codes.append(jnp.where(takers[q] >= 0, takers[q] * 4096 + place, -1))
        in_codes.append((place + (q * 4096 + 1)).astype(F32))
    most_ref[0] = most.astype(jnp.int32)
    mine = lane + (me * NB).astype(F32)
    out_rank = (down(column(source) == mine, column(rank) + 1.0) - 1.0).astype(jnp.int32)
    out_code = jnp.where(me == 0, out_codes[0], jnp.where(me == 1, out_codes[1], -1))
    hit = column(jnp.concatenate(leaves, axis=1)) == mine
    in_code = down(hit, column(jnp.concatenate(in_codes, axis=1))).astype(jnp.int32) - 1
    codes_ref[0:1] = out_rank
    codes_ref[1:2] = out_code
    codes_ref[2:8] = jnp.zeros((6, NB), jnp.int32)
    every_ref[:, :2 * NB] = owner * 4096 + rank.astype(jnp.int32)
    every_ref[:, 2 * NB:] = in_code
    parts = split2(panel_ref[...])
    for c in range(4):
        onehot = blocks_onehot(out_rank, out_code, 4 * c, 4)
        out_ref[4 * c * CAP:4 * (c + 1) * CAP] = pick_t(onehot, parts)


def make_plan(where, pivot_one, pivot_two, panel_t):
    return pl.pallas_call(
        plan_kernel,
        in_specs=[SMEM] + [VMEM] * 3,
        out_specs=[VMEM, VMEM, SMEM, VMEM],
        out_shape=[
            jax.ShapeDtypeStruct((8, NB), jnp.int32),
            jax.ShapeDtypeStruct((1, 3 * NB), jnp.int32),
            jax.ShapeDtypeStruct((1,), jnp.int32),
            jax.ShapeDtypeStruct((SLOTS, 128), F32),
        ],
        name="make_plan",
    )(where, pivot_one.reshape(1, NB), pivot_two.reshape(1, NB), panel_t)


def pack_kernel(codes_ref, rows_ref, out_ref, parts_ref):
    step = pl.program_id(0)

    @pl.when(step == 0)
    def _():
        for n, part in enumerate(split2(rows_ref[...])):
            parts_ref[n] = part

    onehot = blocks_onehot(codes_ref[0:1], codes_ref[1:2], step * 4, 4)
    out_ref[...] = pick(onehot, (parts_ref[0], parts_ref[1], parts_ref[2]))


def pack(codes, rows):
    width = rows.shape[1]
    return pl.pallas_call(
        pack_kernel,
        grid=(4,),
        in_specs=[pl.BlockSpec((8, NB), lambda i: (0, 0)), pl.BlockSpec((NB, width), lambda i: (0, 0))],
        out_specs=pl.BlockSpec((4 * CAP, width), lambda i: (i, 0)),
        out_shape=jax.ShapeDtypeStruct((SLOTS, width), F32),
        scratch_shapes=[pltpu.VMEM((3, NB, width), BF16)],
        name="pack_rows",
    )(codes, rows)


def slots_of(at_ref, n):
    code = at_ref[:, n * NB:(n + 1) * NB]
    place = code & 4095
    at = column(jnp.where(place < CAP, (code >> 12) * SOME + place - n * (CAP - SOME), -1))
    return jnp.where(iota((NB, FEW), 1) == at, 1.0, 0.0).astype(BF16)


def share(got, n):
    some = got[:, :SOME] if n == 0 else got[:, CAP - SOME:]
    return some.reshape(FEW, got.shape[2])


def arrivals(at_ref):
    code = at_ref[:, 2 * NB:]
    at = column(in_first(code))
    return jnp.where(iota((NB, 2 * CAP), 1) == at, 1.0, 0.0).astype(BF16), column(code) >= 0


def late(flag_ref, extra_ref, buffer, sem, first=True):
    @pl.when((flag_ref[0] < CAP) & first)
    def _():
        buffer[...] = jnp.zeros_like(buffer)

    @pl.when(flag_ref[0] >= CAP)
    def _():
        copy = pltpu.make_async_copy(extra_ref, buffer, sem)
        copy.start()
        copy.wait()

    return buffer


def panel_rows_kernel(where_ref, flag_ref, at_ref, got_ref, extra_ref, keep_ref, send_ref, tops_ref, more, sem):
    core = where_ref[1]
    more = late(flag_ref, extra_ref.at[:2 * NB, :128], more, sem)
    got = got_ref[...]
    first = pick(slots_of(at_ref, 0), split2(share(got, 0))) + more[:NB]
    second = pick(slots_of(at_ref, 1), split2(share(got, 1))) + more[NB:]
    left = iota((NB, 128), 1) < 64
    tops_ref[...] = jnp.where(left, first, second)
    swapped = jnp.where(left, second, first)
    upper = swapped[:HALF]
    lower = jnp.concatenate([swapped[HALF:], got[:2].reshape(2 * CAP, 128)], axis=0)
    keep_ref[...] = jnp.where(core == 0, upper, lower)
    send_ref[...] = jnp.where(core == 0, lower, upper)


def panel_rows(where, flag, at, got, extra):
    half = jax.ShapeDtypeStruct((HALF, 128), F32)
    return pl.pallas_call(
        panel_rows_kernel,
        in_specs=[SMEM] * 2 + [VMEM] * 2 + [ANY],
        out_specs=[VMEM] * 3,
        out_shape=[half, half, jax.ShapeDtypeStruct((NB, 128), F32)],
        scratch_shapes=[pltpu.VMEM((2 * NB, 128), F32), pltpu.SemaphoreType.DMA],
        compiler_params=pltpu.CompilerParams(vmem_limit_bytes=GRANT),
        name="panel_rows",
    )(where, flag, at, got, extra)


def fold_kernel(at_ref, lower_ref, one_ref, two_ref):
    for n, out in enumerate((one_ref, two_ref)):
        onehot = slots_of(at_ref, n)
        high, low = split2(lower_ref[n])
        out[0] = mm(high, onehot).astype(BF16)
        out[1] = mm(low, onehot).astype(BF16)


def fold(at, lower_inv):
    shape = jax.ShapeDtypeStruct((2, NB, FEW), BF16)
    return pl.pallas_call(
        fold_kernel, in_specs=[VMEM] * 2, out_specs=[VMEM] * 2, out_shape=[shape, shape], name="fold_slots"
    )(at, lower_inv)


def own_panels_kernel(where_ref, p0, p1, p2, p3, out_ref, gath):
    core, z = where_ref[1], where_ref[2]
    for s, piece in enumerate((p0, p1, p2, p3)):
        zz = lax.rem(z + 4 - s, 4)
        gath[zz, core] = piece[:128]
        gath[zz, 1 - core] = piece[128:]
    for n in range(2):
        half = [gath[c // 2, c % 2, 64 * n:64 * (n + 1)] for c in range(8)]
        out_ref[n] = jnp.transpose(jnp.concatenate(half, axis=0))


def own_panels(where, pieces):
    return pl.pallas_call(
        own_panels_kernel,
        in_specs=[SMEM] + [VMEM] * 4,
        out_specs=VMEM,
        out_shape=jax.ShapeDtypeStruct((2, NB, NB), F32),
        scratch_shapes=[pltpu.VMEM((4, 2, 128, NB), F32)],
        compiler_params=pltpu.CompilerParams(vmem_limit_bytes=GRANT),
        name="own_panels",
    )(where, *pieces)


def panel_math_kernel(where_ref, flag_ref, at_ref, tops_ref, whole_ref, extra_ref, k0, k1, k2, k3, p0, p1, p2, p3,
                      lower_ref, upper_ref, left_ref, pout_ref, gath, src, more, sem):
    me, core, z = where_ref[0], where_ref[1], where_ref[2]
    for s, (a, b) in enumerate(((k0, p0), (k1, p1), (k2, p2), (k3, p3))):
        zz = lax.rem(z + 4 - s, 4)
        gath[core, zz] = a[...]
        gath[1 - core, zz] = b[...]
    more = late(flag_ref, extra_ref, more, sem)
    left = iota((2 * HALF, 128), 1) < 64
    ones, twos = [], []
    for zz in range(4):
        a = jnp.concatenate([gath[0, zz, :HALF], gath[1, zz, HALF:]], axis=0)
        b = jnp.concatenate([gath[0, zz, HALF:], gath[1, zz, :HALF]], axis=0)
        ones.append(jnp.where(left, a, pltpu.roll(b, 64, 1)))
        twos.append(jnp.where(left, pltpu.roll(a, 64, 1), b))
    in_one, in_two = jnp.concatenate(ones, axis=1), jnp.concatenate(twos, axis=1)
    onehot, moved = arrivals(at_ref)
    top_two_one, top_one_two = in_one[:NB], in_two[:NB]
    own_one = jnp.where(moved, pick(onehot, split2(in_one[NB:])) + more[0], whole_ref[0])
    own_two = jnp.where(moved, pick(onehot, split2(in_two[NB:])) + more[1], whole_ref[1])
    own_one = jnp.where(me == 1, top_two_one, own_one)
    own_two = jnp.where(me == 1, 0.0, own_two)
    upper_one_inv = split2(upper_ref[0])
    lower_kept = dot3_upper(split2(own_one), upper_one_inv)
    lower_top = dot3_upper(split2(top_two_one), upper_one_inv)
    upper_panel = dot3_lower(split2(lower_ref[0]), split2(top_one_two))
    kept_parts = split2(lower_kept)
    updated = own_two - dot3(kept_parts, split2(upper_panel))
    lower_two = dot3_upper(split2(updated), split2(upper_ref[1]))
    left_ref[0], left_ref[1] = kept_parts
    left_ref[2], left_ref[3] = split2(lower_two)
    left_ref[4], left_ref[5] = split2(dot3_lower(split2(lower_ref[1]), split2(lower_top)))
    src[0] = lower_kept
    src[1] = jnp.where(me == 0, upper_panel, jnp.where(me == 1, updated, lower_two))
    at = pl.multiple_of(z * 128, 128)
    one = src[0, :, pl.ds(at, 128)]
    two = src[1, :, pl.ds(at, 128)]
    left = iota((NB, 128), 1) < 64
    mine = jnp.where(
        core == 0,
        jnp.where(left, one, pltpu.roll(two, 64, 1)),
        jnp.where(left, pltpu.roll(one, 64, 1), two),
    )
    tops = tops_ref[...]
    mine = jnp.where(left & (me == 0), tops, mine)
    mine = jnp.where(jnp.logical_not(left) & (me == 1), tops + mine, mine)
    pout_ref[...] = jnp.transpose(mine)


def panel_math(where, flag, at, tops, whole, extra, kept, other, lower_inv, upper_inv):
    return pl.pallas_call(
        panel_math_kernel,
        in_specs=[SMEM] * 2 + [VMEM] * 3 + [ANY] + [VMEM] * 10,
        out_specs=[VMEM] * 2,
        out_shape=[jax.ShapeDtypeStruct((6, NB, NB), BF16), jax.ShapeDtypeStruct((128, NB), F32)],
        scratch_shapes=[
            pltpu.VMEM((2, 4, 2 * HALF, 128), F32),
            pltpu.VMEM((2, NB, NB), F32),
            pltpu.VMEM((2, NB, NB), F32),
            pltpu.SemaphoreType.DMA,
        ],
        compiler_params=pltpu.CompilerParams(vmem_limit_bytes=GRANT),
        name="panel_math",
    )(where, flag, at, tops, whole, extra, *kept, *other, lower_inv, upper_inv)


WIDE = 256


def slab_kernel(where_ref, flag_ref, at_ref, got_ref, rows_ref, extra_ref, one_ref, two_ref, left_ref, out_ref,
                more, sem):
    me = where_ref[0]
    at = pl.multiple_of(pl.program_id(0) * WIDE, WIDE)
    more = late(flag_ref, extra_ref.at[:, pl.ds(at, WIDE)], more, sem, pl.program_id(0) == 0)
    got = got_ref[...]
    upper_one = dot3((one_ref[0], one_ref[1]), split2(share(got, 0))) + more[:NB]
    one = split2(upper_one)
    upper_two = (dot3((two_ref[0], two_ref[1]), split2(share(got, 1))) - dot3((left_ref[4], left_ref[5]), one)) + more[NB:2 * NB]

    @pl.when(me == 0)
    def _():
        out_ref[...] = upper_one

    @pl.when(me == 1)
    def _():
        out_ref[...] = upper_two

    @pl.when(me > 1)
    def _():
        onehot, moved = arrivals(at_ref)
        own = jnp.where(moved, pick(onehot, split2(got[:2].reshape(2 * CAP, WIDE))) + more[2 * NB:], rows_ref[...])
        two = split2(upper_two)
        out_ref[...] = own - dot3((left_ref[0], left_ref[1]), one) - dot3((left_ref[2], left_ref[3]), two)


def slab_math(where, flag, at, got, rows, extra, one, two, left):
    whole = lambda *shape: pl.BlockSpec(shape, lambda i: (0,) * len(shape))
    return pl.pallas_call(
        slab_kernel,
        grid=(NB // WIDE,),
        in_specs=[
            SMEM,
            SMEM,
            whole(1, 3 * NB),
            pl.BlockSpec((PEERS, CAP, WIDE), lambda i: (0, 0, i)),
            pl.BlockSpec((NB, WIDE), lambda i: (0, i)),
            ANY,
            whole(2, NB, FEW),
            whole(2, NB, FEW),
            whole(6, NB, NB),
        ],
        out_specs=pl.BlockSpec((NB, WIDE), lambda i: (0, i)),
        out_shape=jax.ShapeDtypeStruct((NB, NB), F32),
        scratch_shapes=[pltpu.VMEM((3 * NB, WIDE), F32), pltpu.SemaphoreType.DMA],
        name="slab_math",
    )(where, flag, at, got, rows, extra, one, two, left)


def exchange(blocks):
    width = blocks.shape[1]
    return lax.all_to_all(blocks.reshape(PEERS, CAP, width), RD, 0, 0)


def unused_kernel(*refs):
    pass


def unwritten(*shapes):
    return pl.pallas_call(
        unused_kernel,
        out_specs=[ANY] * len(shapes),
        out_shape=[jax.ShapeDtypeStruct(shape, F32) for shape in shapes],
        name="unwritten",
    )()


def late_pack_kernel(base_ref, codes_ref, panel_ref, rows_ref, out_ref):
    k = iota((CAP, NB), 0) + base_ref[0]
    picked = (k == codes_ref[0:1]) | ((k + pl.program_id(0) * 4096) == codes_ref[1:2])
    onehot = jnp.where(picked, 1.0, 0.0).astype(BF16)
    out_ref[:, :128] = pick_t(onehot, split2(panel_ref[...]))
    out_ref[:, 128:] = pick(onehot, split2(rows_ref[...]))


def late_pack(base, codes, panel_t, slab):
    whole = lambda *shape: pl.BlockSpec(shape, lambda i: (0,) * len(shape))
    return pl.pallas_call(
        late_pack_kernel,
        grid=(PEERS,),
        in_specs=[SMEM, whole(8, NB), whole(128, NB), whole(NB, NB)],
        out_specs=pl.BlockSpec((CAP, 128 + NB), lambda i: (i, 0)),
        out_shape=jax.ShapeDtypeStruct((SLOTS, 128 + NB), F32),
        name="late_pack",
    )(base, codes, panel_t, slab)


def late_place_kernel(base_ref, every_ref, got_ref, old_ref, out_ref):
    code = column(every_ref[...])
    place = (code & 4095) - base_ref[0]
    now = (code >= 0) & (place >= 0) & (place < CAP)
    at = jnp.where(now, (code >> 12) * CAP + place, -1)
    onehot = jnp.where(iota((128, SLOTS), 1) == at, 1.0, 0.0).astype(BF16)
    old = jnp.where(base_ref[0] == CAP, 0.0, old_ref[...])
    out_ref[...] = jnp.where(now, pick(onehot, split2(got_ref[...])), old)


def late_place(base, every, got, old):
    block = pl.BlockSpec((128, 128 + NB), lambda i: (i, 0))
    return pl.pallas_call(
        late_place_kernel,
        grid=(12,),
        in_specs=[
            SMEM,
            pl.BlockSpec((1, 128), lambda i: (0, i)),
            pl.BlockSpec((SLOTS, 128 + NB), lambda i: (0, 0)),
            block,
        ],
        out_specs=block,
        out_shape=jax.ShapeDtypeStruct((3 * NB, 128 + NB), F32),
        name="late_place",
    )(base, every, got, old)


def late_product_kernel(lower_ref, rows_ref, out_ref):
    n = pl.program_id(0)

    @pl.when(n < 8)
    def _():
        out_ref[...] = dot3(split2(lower_ref[0]), split2(rows_ref[:, 128:]))

    @pl.when(n >= 8)
    def _():
        at = pl.multiple_of(lax.rem(n, 4) * 128, 128)
        out_ref[...] = rows_ref[pl.ds(at, 128), 128:]


def late_product(lower_inv, rows):
    return pl.pallas_call(
        late_product_kernel,
        grid=(12,),
        in_specs=[
            pl.BlockSpec((1, 128, NB), lambda i: (lax.min(i // 4, 1), i % 4, 0)),
            pl.BlockSpec((NB, 128 + NB), lambda i: (i // 4, 0)),
        ],
        out_specs=pl.BlockSpec((128, NB), lambda i: (i, 0)),
        out_shape=jax.ShapeDtypeStruct((3 * NB, NB), F32),
        name="late_product",
    )(lower_inv, rows)


def late_panel_kernel(in_ref, out_ref):
    left = iota((NB, 128), 1) < 64
    a, b = in_ref[0], in_ref[1]
    out_ref[0] = jnp.where(left, a, pltpu.roll(b, 64, 1))
    out_ref[1] = jnp.where(left, pltpu.roll(a, 64, 1), b)


def late_panel(pieces):
    return pl.pallas_call(
        late_panel_kernel,
        grid=(4,),
        in_specs=[pl.BlockSpec((2, NB, 128), lambda i: (i, 0, 0))],
        out_specs=pl.BlockSpec((2, NB, 128), lambda i: (0, 0, i)),
        out_shape=jax.ShapeDtypeStruct((2, NB, NB), F32),
        name="late_panel",
    )(pieces)


def late_exchange(blocks, me):
    ring = [(i, (i + 1) % PEERS) for i in range(PEERS)]

    def turn(t, state):
        held, got = state
        mine = lax.dynamic_slice_in_dim(held, me * CAP, CAP, 0)
        got = lax.dynamic_update_slice_in_dim(got, mine, (me - t) % PEERS * CAP, 0)
        return lax.ppermute(held, RD, ring), got

    return lax.fori_loop(0, PEERS, turn, (blocks, jnp.zeros(blocks.shape, F32)))[1]


def late_gather(rows, col):
    ring = [(i, (i + 1) % 8) for i in range(8)]

    def turn(t, state):
        held, got = state
        got = lax.dynamic_update_slice_in_dim(got, held[None], (col - t) % 8, 0)
        return lax.ppermute(held, "col", ring), got

    return lax.fori_loop(0, 8, turn, (rows, jnp.zeros((8, *rows.shape), F32)))[1]


def further_rounds(most, codes, every, panel_t, slab, lower_inv, me, col):
    def turn(state):
        r, rows = state[:2]
        base = (r * CAP).reshape(1)
        got = late_exchange(late_pack(base, codes, panel_t, slab), me)
        rows = late_place(base, every, got, rows)
        wide = late_panel(late_gather(rows[2 * NB:, :128], col))
        return r + 1, rows, wide, late_product(lower_inv, rows)

    start = (jnp.int32(1), *unwritten((3 * NB, 128 + NB), (2, NB, NB), (3 * NB, NB)))
    return lax.while_loop(lambda s: s[0] * CAP <= most, turn, start)[1:]


def partner(x):
    return lax.ppermute(x, "col", [(c, c ^ 1) for c in range(8)])


def shift(x, by):
    return lax.ppermute(x, "col", [(c, (c // 2 + by) % 4 * 2 + c % 2) for c in range(8)])


def body(panels, slab, pivot_one, pivot_two, lower_inv, upper_inv):
    me = lax.axis_index(RD)
    col = lax.axis_index("col")
    where = jnp.stack([me, col % 2, col // 2, col]).astype(jnp.int32)
    panel_t = jnp.swapaxes(panels, 1, 2).reshape(128, NB)
    panel_pair = jnp.concatenate([panel_t, partner(panel_t)], axis=0)
    codes, every, most, blocks = make_plan(where, pivot_one, pivot_two, panel_t)
    got_panel = exchange(blocks)
    pieces = [panel_pair] + [shift(panel_pair, by) for by in (1, 2, 3)]
    whole = own_panels(where, pieces)
    blocks = pack(codes, slab)
    late_rows, late_own, late_slab = further_rounds(most[0], codes, every, panel_t, slab, lower_inv, me, col)
    got_slab = exchange(blocks)
    keep, send, tops = panel_rows(where, most, every, got_panel, late_rows)
    pair = jnp.concatenate([keep, partner(send)], axis=0)
    shifted = [shift(pair, by) for by in (1, 2, 3)]
    one, two = fold(every, lower_inv)
    shifted, one, two = lax.optimization_barrier((shifted, one, two))
    kept = [pair] + shifted
    other = [partner(x) for x in kept]
    left, panel_out = panel_math(where, most, every, tops, whole, late_own, kept, other, lower_inv, upper_inv)
    slab_out = slab_math(where, most, every, got_slab, slab, late_slab, one, two, left)
    return jnp.swapaxes(panel_out.reshape(2, 64, NB), 1, 2), slab_out


def solution(mesh):
    placed = (P(None, RD, "col"), P(RD, "col"), P(), P(), P(), P())
    return jax.shard_map(
        body,
        mesh=mesh,
        in_specs=placed,
        out_specs=(P(None, RD, "col"), P(RD, "col")),
        check_vma=False,
    )
```
